32 devices in a mesh: group: 4 (over x, core), dev: 8 (over z, y).
Axes of the slice: x: 2, y: 2, z: 4, core: 2. Of those that a mesh axis runs over, the one named last changes fastest.
Arguments:
- features: bfloat16 [131072, 128], P(('group', 'dev')), may hold values from -6 to 6
- coords: bfloat16 [3, 131072], P(None, ('group', 'dev')), may hold values from 0 to 1
- near_pairs: int32 [2, 256], P(None, 'group'), may hold values from 0 to 127, as said below
- parent_two: int32 [512], P(('group', 'dev')), may hold values from 0 to 31, as said below
- parent_three: int32 [128], P('group'), may hold values from 0 to 7
- rates: float32 [4], replicated, may hold values from 6 to 40
- w_near: bfloat16 [128, 128], replicated, may hold values from -0.5 to 0.5
- restrict: bfloat16 [64, 256], replicated, may hold values from -0.375 to 0.375
- w_two: bfloat16 [128, 128], replicated, may hold values from -0.5 to 0.5
- w_three: bfloat16 [128, 128], replicated, may hold values from -0.5 to 0.5
- w_four: bfloat16 [128, 128], replicated, may hold values from -0.5 to 0.5
- coupling: bfloat16 [32, 32], replicated, may hold values from -1 to 1
- expand: bfloat16 [256, 64], replicated, may hold values from -0.75 to 0.75
- w_out: bfloat16 [128, 128], replicated, may hold values from -0.5 to 0.5
Outputs:
- mixed: bfloat16 [131072, 128], P(('group', 'dev'))
The draws below stay inside these ranges and needn't reach their ends.
Inputs may be any that keep to these rules, and one draw needn't show every extreme that they name: `near_pairs`: for any two devices A and P of dev in one region, at most 2 near pairs of that region have their first block on A and their second on P, and in each region some such two devices have exactly 2. `parent_two`: every level-two node of a region is named by exactly four blocks of that region.
All inputs are finite; a program needn't handle non-finite values.
Results may differ from the reference program's by a relative error of at most 0.008.
Values may be sent and summed in bfloat16 or wider, within the bound.
A program may use at most 128 MiB of HBM per device.

```python
import math
import jax
import jax.numpy as jnp
from jax import lax

C = 128
H = 4
B = 256
S = 64
BLK_DEV = 16
CAP = 2
NODES3_GROUP = 8
BLOCKS = 512
POINTS = 131072
BLK_GROUP = 128
PAIRS_GROUP = 64
PAIRS = 256
NODES2_GROUP = 32
NODES2 = 128
NODES3 = 32


def draw_near_pairs(key, part):
    groups_n = PAIRS // PAIRS_GROUP
    devices_n = BLK_GROUP // BLK_DEV
    slots_all = devices_n * devices_n * CAP

    def one_group(group_key):
        keys = jax.random.split(group_key, 5)
        shuffled = jax.random.permutation(keys[0], slots_all).astype(jnp.int32)
        offsets = jax.random.randint(keys[1], (devices_n,), 0, slots_all).astype(jnp.int32)
        slot_ids = jnp.arange(slots_all, dtype=jnp.int32)
        owner_first = slot_ids // (devices_n * CAP)
        owner_second = slot_ids // CAP % devices_n
        score = (shuffled + offsets[owner_first]) * slots_all + slot_ids
        forced = jax.random.randint(keys[2], (), 0, devices_n * devices_n).astype(jnp.int32)
        score = jnp.where(slot_ids // CAP == forced, -1 - slot_ids % CAP, score)
        picked = jnp.argsort(score, stable=True)[:PAIRS_GROUP]
        first_local = jax.random.randint(keys[3], (PAIRS_GROUP,), 0, BLK_DEV).astype(jnp.int32)
        second_local = jax.random.randint(keys[4], (PAIRS_GROUP,), 0, BLK_DEV).astype(jnp.int32)
        first_block = owner_first[picked] * BLK_DEV + first_local
        second_block = owner_second[picked] * BLK_DEV + second_local
        return jnp.stack([first_block, second_block])
    stacked = jax.vmap(one_group)(jax.random.split(jax.random.fold_in(key, 17), groups_n))
    return stacked.transpose(1, 0, 2).reshape(2, PAIRS).astype(jnp.int32)


def draw_parent_two(key, part):
    groups_n = BLOCKS // BLK_GROUP

    def one_group(group_key):
        order = jax.random.permutation(group_key, BLK_GROUP).astype(jnp.int32)
        return order // 4
    stacked = jax.vmap(one_group)(jax.random.split(jax.random.fold_in(key, 23), groups_n))
    return stacked.reshape(BLOCKS).astype(jnp.int32)


def place_ends(array, key, low, high):
    place = [jax.random.randint(jax.random.fold_in(key, axis), (), 0, length) for axis, length in enumerate(array.shape)]
    longest = array.shape.index(max(array.shape))
    next_to = place[:longest] + [(place[longest] + 1) % array.shape[longest]] + place[longest + 1:]
    return array.at[tuple(place)].set(low).at[tuple(next_to)].set(high)


def shard_levels(stream_key, dims, pieces, least, top_value):
    level, own = 1.0, jax.random.fold_in(stream_key, 6)
    for axis_at, parts in pieces:
        heights = jnp.exp(jax.random.uniform(jax.random.fold_in(own, axis_at), (parts,), jnp.float32, least / len(pieces), top_value / len(pieces)))
        level = level * jnp.repeat(heights, dims[axis_at] // parts).reshape([-1 if axis == axis_at else 1 for axis in range(len(dims))])
    return level


def gaussian(key, extent, width, limit, pieces=(), held_as=jnp.bfloat16):
    entries = jax.random.normal(key, extent, jnp.float32) * width
    if len(pieces) > 0:
        entries = shard_levels(key, extent, pieces, -0.22, 0.18) * entries
    return jnp.clip(entries, min=-limit, max=limit).astype(held_as)


def setup_inputs(seed: int = 0) -> dict:
    key_list = jax.random.split(jax.random.key(seed), 15)
    features = gaussian(key_list[0], (POINTS, C), 1.0, 6.0, ((0, 32),))
    coords = jnp.clip(1.0 * jax.random.uniform(key_list[1], (3, POINTS), jnp.float32) ** shard_levels(key_list[1], (3, POINTS), ((1, 32),), -0.2, 0.2), 0.0, 1.0).astype(jnp.bfloat16)
    near_pairs = draw_near_pairs(jax.random.fold_in(key_list[14], 71), 0)
    parent_two = draw_parent_two(jax.random.fold_in(key_list[14], 71), 0)
    parent_three = place_ends(jax.random.randint(key_list[4], (NODES2,), 0, NODES3_GROUP), jax.random.fold_in(key_list[4], 1), 0, NODES3_GROUP - 1).astype(jnp.int32)
    rates = jnp.clip(jnp.exp(jax.random.uniform(key_list[5], (H,), jnp.float32, math.log(6.0), math.log(40.0))), 6.0, 40.0)
    w_near = gaussian(key_list[6], (C, C), C ** -0.5, 0.5)
    restrict = gaussian(key_list[7], (S, B), B ** -0.5, 0.375)
    w_two = gaussian(key_list[8], (C, C), C ** -0.5, 0.5)
    w_three = gaussian(key_list[9], (C, C), C ** -0.5, 0.5)
    w_four = gaussian(key_list[10], (C, C), C ** -0.5, 0.5)
    coupling = gaussian(key_list[11], (NODES3, NODES3), NODES3 ** -0.5, 1.0)
    expand = gaussian(key_list[12], (B, S), S ** -0.5, 0.75)
    w_out = gaussian(key_list[13], (C, C), C ** -0.5, 0.5)
    return dict(features=features, coords=coords, near_pairs=near_pairs, parent_two=parent_two, parent_three=parent_three, rates=rates, w_near=w_near, restrict=restrict, w_two=w_two, w_three=w_three, w_four=w_four, coupling=coupling, expand=expand, w_out=w_out)


def kernel_table(cloud_one, cloud_two, rates):
    first_pos = cloud_one.astype(jnp.float32)
    second_pos = cloud_two.astype(jnp.float32)
    delta_x = first_pos[:, 0, :, None] - second_pos[:, 0, None, :]
    delta_y = first_pos[:, 1, :, None] - second_pos[:, 1, None, :]
    delta_z = first_pos[:, 2, :, None] - second_pos[:, 2, None, :]
    distance = delta_x * delta_x + delta_y * delta_y + delta_z * delta_z
    return jnp.exp(-rates[None, :, None, None] * distance[:, None]).astype(jnp.bfloat16)


def apply_table(kernel, block_values, head_count, transposed):
    blocks_n, points_n, channels = block_values.shape
    by_head = block_values.reshape(blocks_n, points_n, head_count, channels // head_count)
    form = "nhqp,nqhc->nphc" if transposed else "nhpq,nqhc->nphc"
    result = jnp.einsum(form, kernel.astype(jnp.float32), by_head.astype(jnp.float32))
    return result.reshape(blocks_n, points_n, channels)


def reference(features, coords, near_pairs, parent_two, parent_three, rates, w_near, restrict, w_two, w_three, w_four, coupling, expand, w_out):
    head_count = rates.shape[0]
    values = jnp.dot(features, w_near, preferred_element_type=jnp.float32).astype(jnp.bfloat16)
    vblocks = values.reshape(BLOCKS, B, C)
    cblocks = coords.reshape(3, BLOCKS, B).transpose(1, 0, 2)

    def self_term(operands):
        cloud, block_values = operands
        return apply_table(kernel_table(cloud, cloud, rates), block_values, head_count, False)

    near_field = lax.map(self_term, (cblocks.reshape(-1, 8, 3, B), vblocks.reshape(-1, 8, B, C))).reshape(BLOCKS, B, C)
    pair_group = jnp.arange(PAIRS, dtype=jnp.int32) // PAIRS_GROUP
    first_ids = near_pairs[0] + pair_group * BLK_GROUP
    second_ids = near_pairs[1] + pair_group * BLK_GROUP

    def pair_step(running, batch_pairs):
        first_batch, second_batch = batch_pairs
        kernel = kernel_table(cblocks[first_batch], cblocks[second_batch], rates)
        side_first = apply_table(kernel, vblocks[second_batch], head_count, False)
        side_second = apply_table(kernel, vblocks[first_batch], head_count, True)
        side_second = lax.optimization_barrier(side_second.astype(jnp.bfloat16)).astype(jnp.float32)
        running = running.at[first_batch].add(side_first)
        running = running.at[second_batch].add(side_second)
        return running, None

    near_field, _ = lax.scan(pair_step, near_field, (first_ids.reshape(-1, 32), second_ids.reshape(-1, 32)))

    level_one = jnp.einsum("sb,nbc->nsc", restrict.astype(jnp.float32), features.reshape(BLOCKS, B, C).astype(jnp.float32)).astype(jnp.bfloat16)
    block_group = jnp.arange(BLOCKS, dtype=jnp.int32) // BLK_GROUP
    node_two = block_group * NODES2_GROUP + parent_two
    level_two_sum = jax.ops.segment_sum(level_one.astype(jnp.float32), node_two, NODES2).astype(jnp.bfloat16)
    level_two = jax.nn.gelu(jnp.dot(level_two_sum.reshape(-1, C), w_two, preferred_element_type=jnp.float32)).astype(jnp.bfloat16).reshape(NODES2, S, C)
    node_group = jnp.arange(NODES2, dtype=jnp.int32) // NODES2_GROUP
    node_three = node_group * NODES3_GROUP + parent_three
    level_three = (jax.ops.segment_sum(level_two.astype(jnp.float32), node_three, NODES3) * (NODES3_GROUP / NODES2_GROUP)).astype(jnp.bfloat16)
    mixed_three = jnp.dot(coupling, level_three.reshape(NODES3, S * C), preferred_element_type=jnp.float32).astype(jnp.bfloat16)
    down_three = jax.nn.gelu(jnp.dot(mixed_three.reshape(-1, C), w_three, preferred_element_type=jnp.float32)).astype(jnp.bfloat16).reshape(NODES3, S, C)
    lifted = jnp.dot(level_two.reshape(-1, C), w_four, preferred_element_type=jnp.float32).reshape(NODES2, S, C)
    down_two = jax.nn.gelu(lifted + down_three[node_three].astype(jnp.float32)).astype(jnp.bfloat16)
    far_field = jnp.einsum("bs,nsc->nbc", expand.astype(jnp.float32), down_two[node_two].astype(jnp.float32)).astype(jnp.bfloat16)
    total = near_field.reshape(POINTS, C) * (B ** -0.5) + jnp.dot(far_field.reshape(POINTS, C), w_out, preferred_element_type=jnp.float32)
    return total.astype(jnp.bfloat16)
```

```python
import functools
import math

import jax
import jax.numpy as jnp
from jax import lax
from jax.experimental import pallas as pl
from jax.experimental.pallas import tpu as pltpu
from jax.sharding import PartitionSpec as P

CAP = 2
SLOTS = 2 * CAP
AUG = 16
POS = 4
ROWS = 8
LOG2E = math.log2(math.e)
MESH = pl.DeviceIdType.MESH
F32 = jnp.float32
BF16 = jnp.bfloat16


def mm(a, b):
    return jnp.dot(a, b, preferred_element_type=F32)


def iota(shape, axis):
    return lax.broadcasted_iota(jnp.int32, shape, axis)


def onehot(mask):
    return mask.astype(F32).astype(BF16)


def find_slots(n_dev, blocks, pairs_ref, index_ref, prev_ref, last_ref, count_ref):
    me = lax.axis_index("dev")
    pairs_n = pairs_ref.shape[1]

    def clear(i, _):
        index_ref[i] = -1
        return 0

    def clear_count(i, _):
        count_ref[i] = 0
        return 0

    def clear_last(i, _):
        last_ref[i] = i
        return 0

    lax.fori_loop(0, n_dev * SLOTS, clear, 0, unroll=8)
    lax.fori_loop(0, n_dev * 2, clear_count, 0, unroll=8)
    lax.fori_loop(0, blocks, clear_last, 0, unroll=8)

    def one_pair(k, _):
        a = pairs_ref[0, k]
        b = pairs_ref[1, k]
        own_a = lax.div(a, blocks)
        own_b = lax.div(b, blocks)

        @pl.when(own_a == me)
        def _():
            mask = lax.bitwise_xor(own_b, me)
            rank = count_ref[mask]
            index_ref[mask * SLOTS + rank] = a - own_a * blocks
            count_ref[mask] = rank + 1

        @pl.when(own_b == me)
        def _():
            mask = lax.bitwise_xor(own_a, me)
            rank = count_ref[n_dev + mask]
            index_ref[mask * SLOTS + CAP + rank] = b - own_b * blocks
            count_ref[n_dev + mask] = rank + 1

        return 0

    lax.fori_loop(0, pairs_n, one_pair, 0, unroll=4)

    def link(i, place):
        local = index_ref[i]
        prev_ref[place] = 0

        @pl.when(local >= 0)
        def _():
            prev_ref[place] = last_ref[local]
            last_ref[local] = blocks + place

    for slot in range(SLOTS):
        link(slot, slot)
    for slot in range(SLOTS):

        def one(mask, _, slot=slot):
            link(mask * SLOTS + slot, SLOTS + slot * (n_dev - 1) + mask - 1)
            return 0

        lax.fori_loop(1, n_dev, one, 0)


def augment(xyz):
    norm = jnp.sum(xyz * xyz, axis=0, keepdims=True)
    one = norm.astype(BF16).astype(F32)
    two = (norm - one).astype(BF16).astype(F32)
    three = norm - one - two
    ones = jnp.ones_like(norm)
    return (one, two, three), (ones, ones, ones)


def augment_p(xyz):
    norms, ones = augment(xyz)
    pad = jnp.zeros((AUG - 9, xyz.shape[1]), F32)
    return jnp.concatenate((-2.0 * xyz,) + norms + ones + (pad,), axis=0).astype(BF16)


def augment_q(xyz):
    norms, ones = augment(xyz)
    pad = jnp.zeros((AUG - 9, xyz.shape[1]), F32)
    return jnp.concatenate((xyz,) + ones + norms + (pad,), axis=0).astype(BF16)


def table_apply(pos_p, pos_q, values, rates_ref, heads):
    d2 = lax.dot_general(pos_p, pos_q, (((0,), (0,)), ((), ())), preferred_element_type=F32)
    head_of = iota(values.shape, 1) // (values.shape[1] // heads)
    tables, parts = [], []
    for h in range(heads):
        tables.append(jnp.exp2(d2 * (rates_ref[h] * (-LOG2E))).astype(BF16))
        parts.append(jnp.where(head_of == h, values, jnp.zeros_like(values)))
    return mm(jnp.concatenate(tables, axis=1), jnp.concatenate(parts, axis=0))


def exchange(
    n_dev,
    n_group,
    index_ref,
    prev_ref,
    last_ref,
    rates_ref,
    feat_ref,
    coords_ref,
    par_ref,
    p3_ref,
    wnear_ref,
    restrict_ref,
    wtwo_ref,
    wthree_ref,
    wfour_ref,
    coupling_ref,
    expand_ref,
    wout_ref,
    out_ref,
    vals_ref,
    pos4_ref,
    posp_ref,
    send_v,
    got_v,
    send_p,
    got_p,
    running,
    level_ref,
    partial_ref,
    got_part,
    sum_part,
    half_ref,
    lifted_ref,
    three_buf,
    got_three,
    got_down,
    parent_down,
    far_ref,
    v_sems,
    q_sems,
    part_sems,
    three_sems,
    down_sems,
):
    me = lax.axis_index("dev")
    mine = lax.axis_index("group")
    heads = rates_ref.shape[0]
    blocks, points, channels = vals_ref.shape
    s_rows, nodes, _ = partial_ref.shape
    half_n = n_dev // 2
    wide_rows = s_rows // half_n
    nodes3 = coupling_ref.shape[0] // n_group
    stages = n_dev.bit_length() - 1
    bits = [(me // (1 << t)) % 2 for t in range(stages)]

    def peer_of(mask):
        other = 0
        for t in range(stages):
            flip = (mask // (1 << t)) % 2
            other = other + (bits[t] + flip - 2 * bits[t] * flip) * (1 << t)
        return other

    def each(fn, low, high):
        def body(k, _):
            fn(k)
            return 0

        lax.fori_loop(low, high, body, 0)

    barrier = pltpu.get_barrier_semaphore()
    each(
        lambda k: pl.semaphore_signal(barrier, inc=1, device_id={"dev": peer_of(k)}, device_id_type=MESH),
        1,
        n_dev,
    )
    each(
        lambda k: pl.semaphore_signal(
            barrier, inc=1, device_id={"group": (mine + k) % n_group}, device_id_type=MESH
        ),
        1,
        n_group,
    )

    def dev_copy(src, dst, sems, k, mask):
        return pltpu.make_async_remote_copy(
            src_ref=src,
            dst_ref=dst,
            send_sem=sems.at[0, k],
            recv_sem=sems.at[1, k],
            device_id={"dev": peer_of(mask)},
            device_id_type=MESH,
        )

    mine_rows = pl.ds((me % half_n) * wide_rows, wide_rows)

    def near_copy(mask):
        src = partial_ref.at[pl.ds((peer_of(mask) % half_n) * wide_rows, wide_rows)]
        return dev_copy(src, got_part.at[mask], part_sems, mask, mask)

    def across_copy():
        return dev_copy(sum_part.at[0], sum_part.at[1], part_sems, half_n, half_n)

    def down_copy(mask):
        return dev_copy(got_down.at[mine_rows], got_down.at[mine_rows], down_sems, mask, mask)

    def v_copy(mask, slot):
        return dev_copy(send_v.at[mask, slot], got_v.at[mask, slot], v_sems, slot * n_dev + mask, mask)

    def q_copy(mask):
        return dev_copy(send_p.at[mask], got_p.at[mask], q_sems, mask, mask)

    def three_copy(k):
        return pltpu.make_async_remote_copy(
            src_ref=three_buf,
            dst_ref=got_three.at[mine],
            send_sem=three_sems.at[0, k],
            recv_sem=three_sems.at[1, k],
            device_id={"group": (mine + k) % n_group},
            device_id_type=MESH,
        )

    def feed(slot):
        each(lambda k: v_copy(k, slot).start(), half_n, n_dev)
        each(lambda k: v_copy(k, slot).start(), 1, half_n)

    for j in range(blocks):
        xyz = coords_ref[:, j * points : (j + 1) * points].astype(F32)
        pos4_ref[j] = jnp.concatenate([xyz, jnp.zeros((POS - 3, points), F32)], axis=0)
        posp_ref[j] = augment_p(xyz)
        vals_ref[j] = mm(feat_ref[pl.ds(j * points, points), :], wnear_ref[...]).astype(BF16)

    def slot_of(mask, slot):
        return jnp.maximum(index_ref[mask * SLOTS + (slot + CAP) % SLOTS], 0)

    def pick(mask, to_v, to_p):
        for slot in range(SLOTS):
            to_v[mask, slot] = vals_ref[slot_of(mask, slot)]
        to_p[mask] = jnp.concatenate(
            [pos4_ref[slot_of(mask, slot)] for slot in range(SLOTS)], axis=0
        ).astype(BF16)

    pick(0, got_v, got_p)
    each(lambda k: pick(k, send_v, send_p), 1, n_dev)
    pl.semaphore_wait(barrier, n_dev - 1 + n_group - 1)
    feed(0)
    each(lambda k: q_copy(k).start(), 1, n_dev)

    for j in range(blocks):
        level_ref[j] = mm(restrict_ref[...], feat_ref[pl.ds(j * points, points), :]).astype(BF16).astype(F32)
    rows, cols = ROWS * nodes, blocks * ROWS
    row, col = iota((blocks, cols), 0), iota((blocks, cols), 1)
    par_lane = mm(par_ref[...].astype(F32).astype(BF16), onehot(row == col // ROWS)).astype(jnp.int32)
    row, col = iota((rows, cols), 0), iota((rows, cols), 1)
    spread = onehot((row // nodes == col % ROWS) & (row % nodes == par_lane))
    for c in range(s_rows // ROWS):
        part = level_ref[:, c * ROWS : (c + 1) * ROWS, :].reshape(cols, channels).astype(BF16)
        partial_ref[c * ROWS : (c + 1) * ROWS] = mm(spread, part).astype(BF16).reshape(ROWS, nodes, channels)
    each(lambda k: near_copy(k).start(), 1, half_n)

    def self_table(j, _):
        running[j] = table_apply(posp_ref[j], augment_q(pos4_ref[j][:3]), vals_ref[j], rates_ref, heads)
        return 0

    lax.fori_loop(0, blocks, self_table, 0, unroll=2)

    def side_table(mask, slot, place):
        xyz = got_p[mask].astype(F32)[slot * POS : slot * POS + 3]
        local = jnp.maximum(index_ref[mask * SLOTS + slot], 0)
        table = table_apply(posp_ref[local], augment_q(xyz), got_v[mask, slot], rates_ref, heads)
        running[blocks + place] = table + running[prev_ref[place]]

    for slot in range(SLOTS):
        side_table(0, slot, slot)

    def sides(slot, low, high):
        def body(k):
            v_copy(k, slot).wait()
            side_table(k, slot, SLOTS + slot * (n_dev - 1) + k - 1)

        each(body, low, high)

    each(lambda k: near_copy(k).wait(), 1, half_n)
    own = partial_ref[mine_rows].astype(F32)
    for mask in range(1, half_n):
        own = own + got_part[mask].astype(F32)
    half_ref[...] = own
    sum_part[0] = own.astype(BF16)
    across_copy().start()
    feed(1)
    each(lambda k: q_copy(k).wait(), 1, n_dev)
    sides(0, 1, n_dev)

    rows = wide_rows * nodes
    rows3 = wide_rows * nodes3
    all3 = coupling_ref.shape[0]
    row, col = iota((nodes, rows), 0), iota((nodes, rows), 1)
    p3_lane = mm(p3_ref[...].astype(F32).astype(BF16), onehot(row == col % nodes)).astype(jnp.int32)
    row, col = iota((rows3, rows), 0), iota((rows3, rows), 1)
    select = onehot((row // nodes3 == col // nodes) & (row % nodes3 == p3_lane))
    row, col = iota((rows3, all3), 0), iota((rows3, all3), 1)
    left = mm(onehot(col == mine * nodes3 + row % nodes3), coupling_ref[...]).astype(BF16)
    row, col = iota((all3, n_group * rows3), 0), iota((all3, n_group * rows3), 1)
    right = onehot(row == (col // rows3) * nodes3 + col % nodes3)
    row, col = iota((rows3, n_group * rows3), 0), iota((rows3, n_group * rows3), 1)
    wide = jnp.where(row // nodes3 == (col % rows3) // nodes3, mm(left, right), 0.0).astype(BF16)

    across_copy().wait()
    flat = (half_ref[...] + sum_part[1].astype(F32)).reshape(rows, channels).astype(BF16)
    two = jax.nn.gelu(mm(flat, wtwo_ref[...])).astype(BF16)
    three_buf[...] = (mm(select, two) * (nodes3 / nodes)).astype(BF16)
    each(lambda k: three_copy(k).start(), 1, n_group)
    feed(2)
    got_three[mine] = three_buf[...]
    lifted_ref[...] = mm(two, wfour_ref[...])
    each(lambda k: three_copy(k).wait(), 1, n_group)
    mixed = mm(wide, got_three[...].reshape(n_group * rows3, channels)).astype(BF16)
    down3 = jax.nn.gelu(mm(mixed, wthree_ref[...])).astype(BF16)
    lift = lax.dot_general(select, down3, (((0,), (0,)), ((), ())), preferred_element_type=F32)
    got_down[mine_rows] = (
        jax.nn.gelu(lifted_ref[...] + lift).astype(BF16).reshape(wide_rows, nodes, channels)
    )
    each(lambda k: down_copy(k).start(), 1, half_n)
    feed(3)
    sides(1, 1, n_dev)

    def down_wait(mask):
        pltpu.make_async_remote_copy(
            src_ref=got_down.at[mine_rows],
            dst_ref=got_down.at[pl.ds((peer_of(mask) % half_n) * wide_rows, wide_rows)],
            send_sem=down_sems.at[0, mask],
            recv_sem=down_sems.at[1, mask],
            device_id={"dev": peer_of(mask)},
            device_id_type=MESH,
        ).wait()

    each(down_wait, 1, half_n)
    rows, cols = blocks * ROWS, ROWS * nodes
    row, col = iota((rows, blocks), 0), iota((rows, blocks), 1)
    par_wide = jnp.where(row // ROWS == col, par_ref[...].astype(F32), 0.0)
    par_col = jnp.sum(par_wide, axis=1, keepdims=True).astype(jnp.int32)
    row, col = iota((rows, cols), 0), iota((rows, cols), 1)
    gather = onehot((row % ROWS == col // nodes) & (par_col == col % nodes))
    for c in range(s_rows // ROWS):
        part = got_down[c * ROWS : (c + 1) * ROWS].reshape(cols, channels)
        parent_down[:, c * ROWS : (c + 1) * ROWS, :] = mm(gather, part).reshape(blocks, ROWS, channels)
    wide_expand = expand_ref[...].astype(F32).T.astype(BF16)

    for j in range(blocks):
        far = mm(wide_expand, parent_down[j].astype(BF16)).astype(BF16)
        far_ref[j] = mm(far, wout_ref[...])

    sides(2, 1, n_dev)
    sides(3, 1, n_dev)

    for j in range(blocks):
        total = running[last_ref[j]] * (points ** (-0.5)) + far_ref[j]
        out_ref[j * points : (j + 1) * points, :] = total.astype(BF16)


VMEM = pl.BlockSpec(memory_space=pltpu.VMEM)
SMEM = pl.BlockSpec(memory_space=pltpu.SMEM)


def per_device(
    n_dev,
    n_group,
    features,
    coords,
    near_pairs,
    parent_two,
    parent_three,
    rates,
    w_near,
    restrict,
    w_two,
    w_three,
    w_four,
    coupling,
    expand,
    w_out,
):
    points_n, channels = features.shape
    points, s_rows = expand.shape
    blocks = points_n // points
    nodes = parent_three.shape[0]
    slots_n = n_dev * SLOTS
    half_n = n_dev // 2
    wide_rows = s_rows // half_n
    nodes3 = coupling.shape[0] // n_group
    shape = jax.ShapeDtypeStruct
    dma = pltpu.SemaphoreType.DMA
    index, prev, last = pl.pallas_call(
        functools.partial(find_slots, n_dev, blocks),
        out_shape=(
            shape((slots_n,), jnp.int32),
            shape((slots_n,), jnp.int32),
            shape((blocks,), jnp.int32),
        ),
        in_specs=[SMEM],
        out_specs=(SMEM,) * 3,
        scratch_shapes=[pltpu.SMEM((2 * n_dev,), jnp.int32)],
        name="find_slots",
    )(near_pairs)
    return pl.pallas_call(
        functools.partial(exchange, n_dev, n_group),
        out_shape=shape((points_n, channels), BF16),
        in_specs=[SMEM] * 4 + [VMEM] * 12,
        out_specs=VMEM,
        scratch_shapes=[
            pltpu.VMEM((blocks, points, channels), BF16),
            pltpu.VMEM((blocks, POS, points), F32),
            pltpu.VMEM((blocks, AUG, points), BF16),
            pltpu.VMEM((n_dev, SLOTS, points, channels), BF16),
            pltpu.VMEM((n_dev, SLOTS, points, channels), BF16),
            pltpu.VMEM((n_dev, SLOTS * POS, points), BF16),
            pltpu.VMEM((n_dev, SLOTS * POS, points), BF16),
            pltpu.VMEM((blocks + slots_n, points, channels), F32),
            pltpu.VMEM((blocks, s_rows, channels), F32),
            pltpu.VMEM((s_rows, nodes, channels), BF16),
            pltpu.VMEM((half_n, wide_rows, nodes, channels), BF16),
            pltpu.VMEM((2, wide_rows, nodes, channels), BF16),
            pltpu.VMEM((wide_rows, nodes, channels), F32),
            pltpu.VMEM((wide_rows * nodes, channels), F32),
            pltpu.VMEM((wide_rows * nodes3, channels), BF16),
            pltpu.VMEM((n_group, wide_rows * nodes3, channels), BF16),
            pltpu.VMEM((s_rows, nodes, channels), BF16),
            pltpu.VMEM((blocks, s_rows, channels), F32),
            pltpu.VMEM((blocks, points, channels), F32),
            dma((2, SLOTS * n_dev)),
            dma((2, n_dev)),
            dma((2, n_dev)),
            dma((2, n_group)),
            dma((2, n_dev)),
        ],
        compiler_params=pltpu.CompilerParams(
            collective_id=0, has_side_effects=True, vmem_limit_bytes=60 * 1024 * 1024
        ),
        name="exchange",
    )(
        index,
        prev,
        last,
        rates,
        features,
        coords,
        parent_two.reshape(1, -1),
        parent_three.reshape(1, -1),
        w_near,
        restrict,
        w_two,
        w_three,
        w_four,
        coupling,
        expand.T,
        w_out,
    )


def solution(mesh):
    placed = (
        P(("group", "dev"), None),
        P(None, ("group", "dev")),
        P(None, "group"),
        P(("group", "dev")),
        P("group"),
    ) + (P(),) * 9
    return jax.shard_map(
        functools.partial(per_device, mesh.shape["dev"], mesh.shape["group"]),
        mesh=mesh,
        in_specs=placed,
        out_specs=P(("group", "dev"), None),
        check_vma=False,
    )
```

```python
import functools
import math

import jax
import jax.numpy as jnp
from jax import lax
from jax.experimental import pallas as pl
from jax.experimental.pallas import tpu as pltpu
from jax.sharding import PartitionSpec as P

CAP = 2
SLOTS = 2 * CAP
AUG = 16
POS = 4
ROWS = 8
LANES = 128
LOG2E = math.log2(math.e)
MESH = pl.DeviceIdType.MESH
F32 = jnp.float32
BF16 = jnp.bfloat16


def mm(a, b):
    return jnp.dot(a, b, preferred_element_type=F32)


def iota(shape, axis):
    return lax.broadcasted_iota(jnp.int32, shape, axis)


def onehot(mask):
    return mask.astype(F32).astype(BF16)


def find_slots(n_dev, blocks, me, peer_of, pairs):
    pairs_n = pairs.shape[1]
    slots_n = n_dev * SLOTS
    a, b = pairs[0:1], pairs[1:2]

    def slot_and_mask(place):
        remote = place - SLOTS
        slot = jnp.where(remote < 0, place, remote // (n_dev - 1))
        return slot, jnp.where(remote < 0, 0, remote % (n_dev - 1) + 1)

    slot, mask = slot_and_mask(iota((slots_n, 1), 0))
    first = slot < CAP
    here = jnp.where(first, a, b)
    there = jnp.where(first, b, a)
    hit = (here // blocks == me) & (there // blocks == peer_of(mask))
    column = iota((slots_n, pairs_n), 1)
    low = jnp.min(jnp.where(hit, column, pairs_n), axis=1, keepdims=True)
    high = jnp.max(jnp.where(hit, column, -1), axis=1, keepdims=True)
    wanted = jnp.where(slot % CAP == 0, low, jnp.where(high > low, high, pairs_n))
    found = jnp.max(jnp.where(column == wanted, here - me * blocks, -1), axis=1, keepdims=True)

    def to_row(column):
        n = column.shape[0]
        return jnp.max(jnp.where(iota((n, n), 0) == iota((n, n), 1), column, -1), axis=0, keepdims=True)

    found_row = to_row(found)
    place = iota((slots_n, slots_n), 1)
    same = (found_row == found) & (found_row >= 0) & (place < iota((slots_n, slots_n), 0))
    earlier = jnp.max(jnp.where(same, place + blocks, -1), axis=1, keepdims=True)
    prev = jnp.maximum(jnp.where(earlier < 0, found, earlier), 0)
    block = iota((blocks, slots_n), 0)
    last = jnp.where(found_row == block, iota((blocks, slots_n), 1) + blocks, block)
    last = jnp.max(last, axis=1, keepdims=True)
    return jnp.maximum(found_row, 0), to_row(prev), to_row(last)


def augment(xyz):
    norm = jnp.sum(xyz * xyz, axis=0, keepdims=True)
    one = norm.astype(BF16).astype(F32)
    two = (norm - one).astype(BF16).astype(F32)
    three = norm - one - two
    ones = jnp.ones_like(norm)
    return (one, two, three), (ones, ones, ones)


def augment_p(xyz):
    norms, ones = augment(xyz)
    pad = jnp.zeros((AUG - 9, xyz.shape[1]), F32)
    return jnp.concatenate((-2.0 * xyz,) + norms + ones + (pad,), axis=0).astype(BF16)


def augment_q(xyz):
    norms, ones = augment(xyz)
    pad = jnp.zeros((AUG - 9, xyz.shape[1]), F32)
    return jnp.concatenate((xyz,) + ones + norms + (pad,), axis=0).astype(BF16)


def table_apply(pos_p, pos_q, values, rates_ref, heads):
    d2 = lax.dot_general(pos_p, pos_q, (((0,), (0,)), ((), ())), preferred_element_type=F32)
    head_of = iota(values.shape, 1) // (values.shape[1] // heads)
    tables, parts = [], []
    for h in range(heads):
        tables.append(jnp.exp2(d2 * (rates_ref[h] * (-LOG2E))).astype(BF16))
        parts.append(jnp.where(head_of == h, values, jnp.zeros_like(values)))
    return mm(jnp.concatenate(tables, axis=1), jnp.concatenate(parts, axis=0))


def exchange(
    n_dev,
    n_group,
    rates_ref,
    pairs_ref,
    feat_hbm,
    coords_ref,
    par_ref,
    p3_ref,
    wnear_ref,
    restrict_ref,
    wtwo_ref,
    wthree_ref,
    wfour_ref,
    coupling_ref,
    expand_ref,
    wout_ref,
    out_hbm,
    feat_ref,
    out_ref,
    table_ref,
    table_smem,
    vals_ref,
    pos4_ref,
    posp_ref,
    send_v,
    got_v,
    send_p,
    got_p,
    running,
    level_ref,
    partial_ref,
    got_part,
    sum_part,
    half_ref,
    lifted_ref,
    three_buf,
    got_three,
    got_down,
    parent_down,
    far_ref,
    v_sems,
    q_sems,
    part_sems,
    three_sems,
    down_sems,
    local_sems,
    out_sems,
):
    me = lax.axis_index("dev")
    mine = lax.axis_index("group")
    heads = rates_ref.shape[0]
    blocks, points, channels = vals_ref.shape
    s_rows, nodes, _ = partial_ref.shape
    half_n = n_dev // 2
    wide_rows = s_rows // half_n
    nodes3 = coupling_ref.shape[0] // n_group
    stages = n_dev.bit_length() - 1
    bits = [(me // (1 << t)) % 2 for t in range(stages)]

    def peer_of(mask):
        other = 0
        for t in range(stages):
            flip = (mask // (1 << t)) % 2
            other = other + (bits[t] + flip - 2 * bits[t] * flip) * (1 << t)
        return other

    def each(fn, low, high):
        def body(k, _):
            fn(k)
            return 0

        lax.fori_loop(low, high, body, 0)

    barrier = pltpu.get_barrier_semaphore()
    each(
        lambda k: pl.semaphore_signal(barrier, inc=1, device_id={"dev": peer_of(k)}, device_id_type=MESH),
        1,
        n_dev,
    )
    each(
        lambda k: pl.semaphore_signal(
            barrier, inc=1, device_id={"group": (mine + k) % n_group}, device_id_type=MESH
        ),
        1,
        n_group,
    )

    feat_copy = pltpu.make_async_copy(feat_hbm, feat_ref, local_sems.at[0])
    feat_copy.start()

    def dev_copy(src, dst, sems, k, mask):
        return pltpu.make_async_remote_copy(
            src_ref=src,
            dst_ref=dst,
            send_sem=sems.at[0, k],
            recv_sem=sems.at[1, k],
            device_id={"dev": peer_of(mask)},
            device_id_type=MESH,
        )

    mine_rows = pl.ds((me % half_n) * wide_rows, wide_rows)

    def near_copy(mask):
        src = partial_ref.at[pl.ds((peer_of(mask) % half_n) * wide_rows, wide_rows)]
        return dev_copy(src, got_part.at[mask], part_sems, mask, mask)

    def across_copy():
        return dev_copy(sum_part.at[0], sum_part.at[1], part_sems, half_n, half_n)

    def down_copy(mask):
        return dev_copy(got_down.at[mine_rows], got_down.at[mine_rows], down_sems, mask, mask)

    def v_copy(mask, slot):
        return dev_copy(send_v.at[mask, slot], got_v.at[mask, slot], v_sems, slot * n_dev + mask, mask)

    def q_copy(mask):
        return dev_copy(send_p.at[mask], got_p.at[mask], q_sems, mask, mask)

    def three_copy(k):
        return pltpu.make_async_remote_copy(
            src_ref=three_buf,
            dst_ref=got_three.at[mine],
            send_sem=three_sems.at[0, k],
            recv_sem=three_sems.at[1, k],
            device_id={"group": (mine + k) % n_group},
            device_id_type=MESH,
        )

    def feed(slot):
        each(lambda k: v_copy(k, slot).start(), half_n, n_dev)
        each(lambda k: v_copy(k, slot).start(), 1, half_n)

    found = find_slots(n_dev, blocks, me, peer_of, pairs_ref[...])
    table_ref[...] = jnp.zeros_like(table_ref)
    for i, row in enumerate(found):
        table_ref[i : i + 1, : row.shape[1]] = row
    table_copy = pltpu.make_async_copy(table_ref, table_smem, local_sems.at[1])
    table_copy.start()

    for j in range(blocks):
        xyz = coords_ref[:, j * points : (j + 1) * points].astype(F32)
        pos4_ref[j] = jnp.concatenate([xyz, jnp.zeros((POS - 3, points), F32)], axis=0)
        posp_ref[j] = augment_p(xyz)

    table_copy.wait()
    feat_copy.wait()

    def place_of(mask, slot):
        return slot if isinstance(mask, int) and mask == 0 else SLOTS + slot * (n_dev - 1) + mask - 1

    def slot_of(mask, slot):
        return table_smem[0, place_of(mask, (slot + CAP) % SLOTS)]

    def pick_v(mask, slot, to_v):
        to_v[mask, slot] = mm(feat_ref[slot_of(mask, slot)], wnear_ref[...]).astype(BF16)

    def pick_p(mask, to_p):
        to_p[mask] = jnp.concatenate(
            [pos4_ref[slot_of(mask, slot)] for slot in range(SLOTS)], axis=0
        ).astype(BF16)

    each(lambda k: pick_v(k, 0, send_v), half_n, n_dev)
    for j in range(blocks):
        level_ref[j] = mm(restrict_ref[...], feat_ref[j]).astype(BF16).astype(F32)
    rows, cols = ROWS * nodes, blocks * ROWS
    row, col = iota((blocks, cols), 0), iota((blocks, cols), 1)
    par_lane = mm(par_ref[...].astype(F32).astype(BF16), onehot(row == col // ROWS)).astype(jnp.int32)
    row, col = iota((rows, cols), 0), iota((rows, cols), 1)
    spread = onehot((row // nodes == col % ROWS) & (row % nodes == par_lane))
    for c in range(s_rows // ROWS):
        part = level_ref[:, c * ROWS : (c + 1) * ROWS, :].reshape(cols, channels).astype(BF16)
        partial_ref[c * ROWS : (c + 1) * ROWS] = mm(spread, part).astype(BF16).reshape(ROWS, nodes, channels)

    pl.semaphore_wait(barrier, n_dev - 1 + n_group - 1)
    each(lambda k: v_copy(k, 0).start(), half_n, n_dev)
    each(lambda k: near_copy(k).start(), 1, half_n)
    each(lambda k: pick_p(k, send_p), 1, n_dev)
    each(lambda k: q_copy(k).start(), 1, n_dev)
    each(lambda k: pick_v(k, 0, send_v), 1, half_n)
    each(lambda k: v_copy(k, 0).start(), 1, half_n)
    for slot in range(1, SLOTS):
        each(lambda k, slot=slot: pick_v(k, slot, send_v), 1, n_dev)
    for slot in range(SLOTS):
        pick_v(0, slot, got_v)
    pick_p(0, got_p)
    for j in range(blocks):
        vals_ref[j] = mm(feat_ref[j], wnear_ref[...]).astype(BF16)

    def self_table(j, _):
        running[j] = table_apply(posp_ref[j], augment_q(pos4_ref[j][:3]), vals_ref[j], rates_ref, heads)
        return 0

    lax.fori_loop(0, blocks, self_table, 0, unroll=2)

    def side_table(mask, slot, place):
        xyz = got_p[mask].astype(F32)[slot * POS : slot * POS + 3]
        local = table_smem[0, place]
        table = table_apply(posp_ref[local], augment_q(xyz), got_v[mask, slot], rates_ref, heads)
        running[blocks + place] = table + running[table_smem[1, place]]

    for slot in range(SLOTS):
        side_table(0, slot, slot)

    def sides(slot, low, high):
        def body(k):
            v_copy(k, slot).wait()
            side_table(k, slot, place_of(k, slot))

        each(body, low, high)

    each(lambda k: near_copy(k).wait(), 1, half_n)
    own = partial_ref[mine_rows].astype(F32)
    for mask in range(1, half_n):
        own = own + got_part[mask].astype(F32)
    half_ref[...] = own
    sum_part[0] = own.astype(BF16)
    across_copy().start()
    feed(1)
    each(lambda k: q_copy(k).wait(), 1, n_dev)
    sides(0, 1, n_dev)

    rows = wide_rows * nodes
    rows3 = wide_rows * nodes3
    all3 = coupling_ref.shape[0]
    row, col = iota((nodes, rows), 0), iota((nodes, rows), 1)
    p3_lane = mm(p3_ref[...].astype(F32).astype(BF16), onehot(row == col % nodes)).astype(jnp.int32)
    row, col = iota((rows3, rows), 0), iota((rows3, rows), 1)
    select = onehot((row // nodes3 == col // nodes) & (row % nodes3 == p3_lane))
    row, col = iota((rows3, all3), 0), iota((rows3, all3), 1)
    left = mm(onehot(col == mine * nodes3 + row % nodes3), coupling_ref[...]).astype(BF16)
    row, col = iota((all3, n_group * rows3), 0), iota((all3, n_group * rows3), 1)
    right = onehot(row == (col // rows3) * nodes3 + col % nodes3)
    row, col = iota((rows3, n_group * rows3), 0), iota((rows3, n_group * rows3), 1)
    wide = jnp.where(row // nodes3 == (col % rows3) // nodes3, mm(left, right), 0.0).astype(BF16)

    across_copy().wait()
    flat = (half_ref[...] + sum_part[1].astype(F32)).reshape(rows, channels).astype(BF16)
    two = jax.nn.gelu(mm(flat, wtwo_ref[...])).astype(BF16)
    three_buf[...] = (mm(select, two) * (nodes3 / nodes)).astype(BF16)
    each(lambda k: three_copy(k).start(), 1, n_group)
    feed(2)
    got_three[mine] = three_buf[...]
    lifted_ref[...] = mm(two, wfour_ref[...])
    each(lambda k: three_copy(k).wait(), 1, n_group)
    mixed = mm(wide, got_three[...].reshape(n_group * rows3, channels)).astype(BF16)
    down3 = jax.nn.gelu(mm(mixed, wthree_ref[...])).astype(BF16)
    lift = lax.dot_general(select, down3, (((0,), (0,)), ((), ())), preferred_element_type=F32)
    got_down[mine_rows] = (
        jax.nn.gelu(lifted_ref[...] + lift).astype(BF16).reshape(wide_rows, nodes, channels)
    )
    each(lambda k: down_copy(k).start(), 1, half_n)
    feed(3)
    sides(1, 1, n_dev)

    def down_wait(mask):
        pltpu.make_async_remote_copy(
            src_ref=got_down.at[mine_rows],
            dst_ref=got_down.at[pl.ds((peer_of(mask) % half_n) * wide_rows, wide_rows)],
            send_sem=down_sems.at[0, mask],
            recv_sem=down_sems.at[1, mask],
            device_id={"dev": peer_of(mask)},
            device_id_type=MESH,
        ).wait()

    each(down_wait, 1, half_n)
    rows, cols = blocks * ROWS, ROWS * nodes
    row, col = iota((rows, blocks), 0), iota((rows, blocks), 1)
    par_wide = jnp.where(row // ROWS == col, par_ref[...].astype(F32), 0.0)
    par_col = jnp.sum(par_wide, axis=1, keepdims=True).astype(jnp.int32)
    row, col = iota((rows, cols), 0), iota((rows, cols), 1)
    gather = onehot((row % ROWS == col // nodes) & (par_col == col % nodes))
    for c in range(s_rows // ROWS):
        part = got_down[c * ROWS : (c + 1) * ROWS].reshape(cols, channels)
        parent_down[:, c * ROWS : (c + 1) * ROWS, :] = mm(gather, part).reshape(blocks, ROWS, channels)
    wide_expand = expand_ref[...].astype(F32).T.astype(BF16)

    for j in range(blocks):
        far = mm(wide_expand, parent_down[j].astype(BF16)).astype(BF16)
        far_ref[j] = mm(far, wout_ref[...])

    sides(2, 1, n_dev)
    sides(3, 1, n_dev)

    def out_copy(j):
        return pltpu.make_async_copy(
            out_ref.at[j], out_hbm.at[pl.ds(j * points, points)], out_sems.at[j]
        )

    for j in range(blocks):
        total = running[table_smem[2, j]] * (points ** (-0.5)) + far_ref[j]
        out_ref[j] = total.astype(BF16)
        out_copy(j).start()
    for j in range(blocks):
        out_copy(j).wait()


ANY = pl.BlockSpec(memory_space=pl.ANY)
VMEM = pl.BlockSpec(memory_space=pltpu.VMEM)
SMEM = pl.BlockSpec(memory_space=pltpu.SMEM)


def per_device(
    n_dev,
    n_group,
    features,
    coords,
    near_pairs,
    parent_two,
    parent_three,
    rates,
    w_near,
    restrict,
    w_two,
    w_three,
    w_four,
    coupling,
    expand,
    w_out,
):
    points_n, channels = features.shape
    points, s_rows = expand.shape
    blocks = points_n // points
    nodes = parent_three.shape[0]
    slots_n = n_dev * SLOTS
    wide_lanes = -(-slots_n // LANES) * LANES
    half_n = n_dev // 2
    wide_rows = s_rows // half_n
    nodes3 = coupling.shape[0] // n_group
    shape = jax.ShapeDtypeStruct
    dma = pltpu.SemaphoreType.DMA
    return pl.pallas_call(
        functools.partial(exchange, n_dev, n_group),
        out_shape=shape((points_n, channels), BF16),
        in_specs=[SMEM, VMEM, ANY] + [VMEM] * 11,
        out_specs=ANY,
        scratch_shapes=[
            pltpu.VMEM((blocks, points, channels), BF16),
            pltpu.VMEM((blocks, points, channels), BF16),
            pltpu.VMEM((ROWS, wide_lanes), jnp.int32),
            pltpu.SMEM((ROWS, wide_lanes), jnp.int32),
            pltpu.VMEM((blocks, points, channels), BF16),
            pltpu.VMEM((blocks, POS, points), F32),
            pltpu.VMEM((blocks, AUG, points), BF16),
            pltpu.VMEM((n_dev, SLOTS, points, channels), BF16),
            pltpu.VMEM((n_dev, SLOTS, points, channels), BF16),
            pltpu.VMEM((n_dev, SLOTS * POS, points), BF16),
            pltpu.VMEM((n_dev, SLOTS * POS, points), BF16),
            pltpu.VMEM((blocks + slots_n, points, channels), F32),
            pltpu.VMEM((blocks, s_rows, channels), F32),
            pltpu.VMEM((s_rows, nodes, channels), BF16),
            pltpu.VMEM((half_n, wide_rows, nodes, channels), BF16),
            pltpu.VMEM((2, wide_rows, nodes, channels), BF16),
            pltpu.VMEM((wide_rows, nodes, channels), F32),
            pltpu.VMEM((wide_rows * nodes, channels), F32),
            pltpu.VMEM((wide_rows * nodes3, channels), BF16),
            pltpu.VMEM((n_group, wide_rows * nodes3, channels), BF16),
            pltpu.VMEM((s_rows, nodes, channels), BF16),
            pltpu.VMEM((blocks, s_rows, channels), F32),
            pltpu.VMEM((blocks, points, channels), F32),
            dma((2, SLOTS * n_dev)),
            dma((2, n_dev)),
            dma((2, n_dev)),
            dma((2, n_group)),
            dma((2, n_dev)),
            dma((2,)),
            dma((blocks,)),
        ],
        compiler_params=pltpu.CompilerParams(
            collective_id=0, has_side_effects=True, vmem_limit_bytes=60 * 1024 * 1024
        ),
        name="exchange",
    )(
        rates,
        near_pairs,
        features.reshape(blocks, points, channels),
        coords,
        parent_two.reshape(1, -1),
        parent_three.reshape(1, -1),
        w_near,
        restrict,
        w_two,
        w_three,
        w_four,
        coupling,
        expand.T,
        w_out,
    )


def solution(mesh):
    placed = (
        P(("group", "dev"), None),
        P(None, ("group", "dev")),
        P(None, "group"),
        P(("group", "dev")),
        P("group"),
    ) + (P(),) * 9
    return jax.shard_map(
        functools.partial(per_device, mesh.shape["dev"], mesh.shape["group"]),
        mesh=mesh,
        in_specs=placed,
        out_specs=P(("group", "dev"), None),
        check_vma=False,
    )
```

```python
import functools
import math

import jax
import jax.numpy as jnp
from jax import lax
from jax.experimental import pallas as pl
from jax.experimental.pallas import tpu as pltpu
from jax.sharding import PartitionSpec as P

CAP = 2
SLOTS = 2 * CAP
AUG = 16
POS = 4
ROWS = 8
LANES = 128
LOG2E = math.log2(math.e)
MESH = pl.DeviceIdType.MESH
F32 = jnp.float32
BF16 = jnp.bfloat16


def mm(a, b):
    return jnp.dot(a, b, preferred_element_type=F32)


def iota(shape, axis):
    return lax.broadcasted_iota(jnp.int32, shape, axis)


def onehot(mask):
    return mask.astype(F32).astype(BF16)


def find_slots(n_dev, blocks, me, peer_of, pairs):
    pairs_n = pairs.shape[1]
    slots_n = n_dev * SLOTS
    a, b = pairs[0:1], pairs[1:2]

    def slot_and_mask(place):
        remote = place - SLOTS
        slot = jnp.where(remote < 0, place, remote // (n_dev - 1))
        return slot, jnp.where(remote < 0, 0, remote % (n_dev - 1) + 1)

    slot, mask = slot_and_mask(iota((slots_n, 1), 0))
    first = slot < CAP
    here = jnp.where(first, a, b)
    there = jnp.where(first, b, a)
    hit = (here // blocks == me) & (there // blocks == peer_of(mask))
    column = iota((slots_n, pairs_n), 1)
    low = jnp.min(jnp.where(hit, column, pairs_n), axis=1, keepdims=True)
    high = jnp.max(jnp.where(hit, column, -1), axis=1, keepdims=True)
    wanted = jnp.where(slot % CAP == 0, low, jnp.where(high > low, high, pairs_n))
    found = jnp.max(jnp.where(column == wanted, here - me * blocks, -1), axis=1, keepdims=True)

    def to_row(column):
        n = column.shape[0]
        return jnp.max(jnp.where(iota((n, n), 0) == iota((n, n), 1), column, -1), axis=0, keepdims=True)

    found_row = to_row(found)
    place = iota((slots_n, slots_n), 1)
    same = (found_row == found) & (found_row >= 0) & (place < iota((slots_n, slots_n), 0))
    earlier = jnp.max(jnp.where(same, place + blocks, -1), axis=1, keepdims=True)
    prev = jnp.maximum(jnp.where(earlier < 0, found, earlier), 0)
    block = iota((blocks, slots_n), 0)
    last = jnp.where(found_row == block, iota((blocks, slots_n), 1) + blocks, block)
    last = jnp.max(last, axis=1, keepdims=True)
    return jnp.maximum(found_row, 0), to_row(prev), to_row(last)


def augment(xyz):
    norm = jnp.sum(xyz * xyz, axis=0, keepdims=True)
    one = norm.astype(BF16).astype(F32)
    two = (norm - one).astype(BF16).astype(F32)
    three = norm - one - two
    ones = jnp.ones_like(norm)
    return (one, two, three), (ones, ones, ones)


def augment_p(xyz):
    norms, ones = augment(xyz)
    pad = jnp.zeros((AUG - 9, xyz.shape[1]), F32)
    return jnp.concatenate((-2.0 * xyz,) + norms + ones + (pad,), axis=0).astype(BF16)


def augment_q(xyz):
    norms, ones = augment(xyz)
    pad = jnp.zeros((AUG - 9, xyz.shape[1]), F32)
    return jnp.concatenate((xyz,) + ones + norms + (pad,), axis=0).astype(BF16)


def table_apply(pos_p, pos_q, values, rates_ref, heads):
    d2 = lax.dot_general(pos_p, pos_q, (((0,), (0,)), ((), ())), preferred_element_type=F32)
    head_of = iota(values.shape, 1) // (values.shape[1] // heads)
    tables, parts = [], []
    for h in range(heads):
        tables.append(jnp.exp2(d2 * (rates_ref[h] * (-LOG2E))).astype(BF16))
        parts.append(jnp.where(head_of == h, values, jnp.zeros_like(values)))
    return mm(jnp.concatenate(tables, axis=1), jnp.concatenate(parts, axis=0))


def exchange(
    n_dev,
    n_group,
    rates_ref,
    pairs_ref,
    feat_hbm,
    coords_ref,
    par_ref,
    p3_ref,
    wnear_ref,
    restrict_ref,
    wtwo_ref,
    wthree_ref,
    wfour_ref,
    coupling_ref,
    expand_ref,
    wout_ref,
    out_ref,
    feat_ref,
    table_ref,
    table_smem,
    vals_ref,
    pos4_ref,
    posp_ref,
    send_v,
    got_v,
    send_p,
    got_p,
    running,
    level_ref,
    partial_ref,
    got_part,
    sum_part,
    half_ref,
    lifted_ref,
    three_buf,
    got_three,
    got_down,
    parent_down,
    far_ref,
    v_sems,
    q_sems,
    part_sems,
    three_sems,
    down_sems,
    local_sems,
):
    me = lax.axis_index("dev")
    mine = lax.axis_index("group")
    heads = rates_ref.shape[0]
    blocks, points, channels = vals_ref.shape
    s_rows, nodes, _ = partial_ref.shape
    half_n = n_dev // 2
    wide_rows = s_rows // half_n
    nodes3 = coupling_ref.shape[0] // n_group
    stages = n_dev.bit_length() - 1
    bits = [(me // (1 << t)) % 2 for t in range(stages)]

    def peer_of(mask):
        other = 0
        for t in range(stages):
            flip = (mask // (1 << t)) % 2
            other = other + (bits[t] + flip - 2 * bits[t] * flip) * (1 << t)
        return other

    def each(fn, low, high):
        def body(k, _):
            fn(k)
            return 0

        lax.fori_loop(low, high, body, 0)

    barrier = pltpu.get_barrier_semaphore()
    each(
        lambda k: pl.semaphore_signal(barrier, inc=1, device_id={"dev": peer_of(k)}, device_id_type=MESH),
        1,
        n_dev,
    )
    each(
        lambda k: pl.semaphore_signal(
            barrier, inc=1, device_id={"group": (mine + k) % n_group}, device_id_type=MESH
        ),
        1,
        n_group,
    )

    feat_copy = pltpu.make_async_copy(feat_hbm, feat_ref, local_sems.at[0])
    feat_copy.start()

    def dev_copy(src, dst, sems, k, mask):
        return pltpu.make_async_remote_copy(
            src_ref=src,
            dst_ref=dst,
            send_sem=sems.at[0, k],
            recv_sem=sems.at[1, k],
            device_id={"dev": peer_of(mask)},
            device_id_type=MESH,
        )

    mine_rows = pl.ds((me % half_n) * wide_rows, wide_rows)

    def near_copy(mask):
        src = partial_ref.at[pl.ds((peer_of(mask) % half_n) * wide_rows, wide_rows)]
        return dev_copy(src, got_part.at[mask], part_sems, mask, mask)

    def across_copy():
        return dev_copy(sum_part.at[0], sum_part.at[1], part_sems, half_n, half_n)

    def down_copy(mask):
        return dev_copy(got_down.at[mine_rows], got_down.at[mine_rows], down_sems, mask, mask)

    def v_copy(mask, slot):
        return dev_copy(send_v.at[mask, slot], got_v.at[mask, slot], v_sems, slot * n_dev + mask, mask)

    def q_copy(mask):
        return dev_copy(send_p.at[mask], got_p.at[mask], q_sems, mask, mask)

    def three_copy(k):
        return pltpu.make_async_remote_copy(
            src_ref=three_buf,
            dst_ref=got_three.at[mine],
            send_sem=three_sems.at[0, k],
            recv_sem=three_sems.at[1, k],
            device_id={"group": (mine + k) % n_group},
            device_id_type=MESH,
        )

    def feed(slot):
        each(lambda k: v_copy(k, slot).start(), half_n, n_dev)
        each(lambda k: v_copy(k, slot).start(), 1, half_n)

    found = find_slots(n_dev, blocks, me, peer_of, pairs_ref[...])
    table_ref[...] = jnp.zeros_like(table_ref)
    for i, row in enumerate(found):
        table_ref[i : i + 1, : row.shape[1]] = row
    table_copy = pltpu.make_async_copy(table_ref, table_smem, local_sems.at[1])
    table_copy.start()

    for j in range(blocks):
        xyz = coords_ref[:, j * points : (j + 1) * points].astype(F32)
        pos4_ref[j] = jnp.concatenate([xyz, jnp.zeros((POS - 3, points), F32)], axis=0)
        posp_ref[j] = augment_p(xyz)

    table_copy.wait()
    feat_copy.wait()

    def place_of(mask, slot):
        return slot if isinstance(mask, int) and mask == 0 else SLOTS + slot * (n_dev - 1) + mask - 1

    def slot_of(mask, slot):
        return table_smem[0, place_of(mask, (slot + CAP) % SLOTS)]

    def pick_v(mask, slot, to_v):
        to_v[mask, slot] = mm(feat_ref[slot_of(mask, slot)], wnear_ref[...]).astype(BF16)

    def pick_p(mask, to_p):
        to_p[mask] = jnp.concatenate(
            [pos4_ref[slot_of(mask, slot)] for slot in range(SLOTS)], axis=0
        ).astype(BF16)

    each(lambda k: pick_v(k, 0, send_v), half_n, n_dev)
    for j in range(blocks):
        level_ref[j] = mm(restrict_ref[...], feat_ref[j]).astype(BF16).astype(F32)
    rows, cols = ROWS * nodes, blocks * ROWS
    row, col = iota((blocks, cols), 0), iota((blocks, cols), 1)
    par_lane = mm(par_ref[...].astype(F32).astype(BF16), onehot(row == col // ROWS)).astype(jnp.int32)
    row, col = iota((rows, cols), 0), iota((rows, cols), 1)
    spread = onehot((row // nodes == col % ROWS) & (row % nodes == par_lane))
    for c in range(s_rows // ROWS):
        part = level_ref[:, c * ROWS : (c + 1) * ROWS, :].reshape(cols, channels).astype(BF16)
        partial_ref[c * ROWS : (c + 1) * ROWS] = mm(spread, part).astype(BF16).reshape(ROWS, nodes, channels)

    pl.semaphore_wait(barrier, n_dev - 1 + n_group - 1)
    each(lambda k: v_copy(k, 0).start(), half_n, n_dev)
    each(lambda k: near_copy(k).start(), 1, half_n)
    each(lambda k: pick_p(k, send_p), 1, n_dev)
    each(lambda k: q_copy(k).start(), 1, n_dev)
    each(lambda k: pick_v(k, 0, send_v), 1, half_n)
    each(lambda k: v_copy(k, 0).start(), 1, half_n)
    for slot in range(1, SLOTS):
        each(lambda k, slot=slot: pick_v(k, slot, send_v), 1, n_dev)
    for slot in range(SLOTS):
        pick_v(0, slot, got_v)
    pick_p(0, got_p)
    for j in range(blocks):
        vals_ref[j] = mm(feat_ref[j], wnear_ref[...]).astype(BF16)

    def self_table(j, _):
        running[j] = table_apply(posp_ref[j], augment_q(pos4_ref[j][:3]), vals_ref[j], rates_ref, heads)
        return 0

    lax.fori_loop(0, blocks, self_table, 0, unroll=2)

    def side_table(mask, slot, place):
        xyz = got_p[mask].astype(F32)[slot * POS : slot * POS + 3]
        local = table_smem[0, place]
        table = table_apply(posp_ref[local], augment_q(xyz), got_v[mask, slot], rates_ref, heads)
        running[blocks + place] = table + running[table_smem[1, place]]

    for slot in range(SLOTS):
        side_table(0, slot, slot)

    def sides(slot, low, high):
        def body(k):
            v_copy(k, slot).wait()
            side_table(k, slot, place_of(k, slot))

        each(body, low, high)

    each(lambda k: near_copy(k).wait(), 1, half_n)
    own = partial_ref[mine_rows].astype(F32)
    for mask in range(1, half_n):
        own = own + got_part[mask].astype(F32)
    half_ref[...] = own
    sum_part[0] = own.astype(BF16)
    across_copy().start()
    feed(1)
    each(lambda k: q_copy(k).wait(), 1, n_dev)
    sides(0, 1, n_dev)

    rows = wide_rows * nodes
    rows3 = wide_rows * nodes3
    all3 = coupling_ref.shape[0]
    row, col = iota((nodes, rows), 0), iota((nodes, rows), 1)
    p3_lane = mm(p3_ref[...].astype(F32).astype(BF16), onehot(row == col % nodes)).astype(jnp.int32)
    row, col = iota((rows3, rows), 0), iota((rows3, rows), 1)
    select = onehot((row // nodes3 == col // nodes) & (row % nodes3 == p3_lane))
    row, col = iota((rows3, all3), 0), iota((rows3, all3), 1)
    left = mm(onehot(col == mine * nodes3 + row % nodes3), coupling_ref[...]).astype(BF16)
    row, col = iota((all3, n_group * rows3), 0), iota((all3, n_group * rows3), 1)
    right = onehot(row == (col // rows3) * nodes3 + col % nodes3)
    row, col = iota((rows3, n_group * rows3), 0), iota((rows3, n_group * rows3), 1)
    wide = jnp.where(row // nodes3 == (col % rows3) // nodes3, mm(left, right), 0.0).astype(BF16)

    across_copy().wait()
    flat = (half_ref[...] + sum_part[1].astype(F32)).reshape(rows, channels).astype(BF16)
    two = jax.nn.gelu(mm(flat, wtwo_ref[...])).astype(BF16)
    three_buf[...] = (mm(select, two) * (nodes3 / nodes)).astype(BF16)
    each(lambda k: three_copy(k).start(), 1, n_group)
    feed(2)
    got_three[mine] = three_buf[...]
    lifted_ref[...] = mm(two, wfour_ref[...])
    each(lambda k: three_copy(k).wait(), 1, n_group)
    mixed = mm(wide, got_three[...].reshape(n_group * rows3, channels)).astype(BF16)
    down3 = jax.nn.gelu(mm(mixed, wthree_ref[...])).astype(BF16)
    lift = lax.dot_general(select, down3, (((0,), (0,)), ((), ())), preferred_element_type=F32)
    got_down[mine_rows] = (
        jax.nn.gelu(lifted_ref[...] + lift).astype(BF16).reshape(wide_rows, nodes, channels)
    )
    each(lambda k: down_copy(k).start(), 1, half_n)
    feed(3)
    sides(1, 1, n_dev)

    def down_wait(mask):
        pltpu.make_async_remote_copy(
            src_ref=got_down.at[mine_rows],
            dst_ref=got_down.at[pl.ds((peer_of(mask) % half_n) * wide_rows, wide_rows)],
            send_sem=down_sems.at[0, mask],
            recv_sem=down_sems.at[1, mask],
            device_id={"dev": peer_of(mask)},
            device_id_type=MESH,
        ).wait()

    each(down_wait, 1, half_n)
    rows, cols = blocks * ROWS, ROWS * nodes
    row, col = iota((rows, blocks), 0), iota((rows, blocks), 1)
    par_wide = jnp.where(row // ROWS == col, par_ref[...].astype(F32), 0.0)
    par_col = jnp.sum(par_wide, axis=1, keepdims=True).astype(jnp.int32)
    row, col = iota((rows, cols), 0), iota((rows, cols), 1)
    gather = onehot((row % ROWS == col // nodes) & (par_col == col % nodes))
    for c in range(s_rows // ROWS):
        part = got_down[c * ROWS : (c + 1) * ROWS].reshape(cols, channels)
        parent_down[:, c * ROWS : (c + 1) * ROWS, :] = mm(gather, part).reshape(blocks, ROWS, channels)
    wide_expand = expand_ref[...].astype(F32).T.astype(BF16)

    for j in range(blocks):
        far = mm(wide_expand, parent_down[j].astype(BF16)).astype(BF16)
        far_ref[j] = mm(far, wout_ref[...])

    sides(2, 1, n_dev)
    sides(3, 1, n_dev)

    for j in range(blocks):
        total = running[table_smem[2, j]] * (points ** (-0.5)) + far_ref[j]
        out_ref[j] = total.astype(BF16)


ANY = pl.BlockSpec(memory_space=pl.ANY)
VMEM = pl.BlockSpec(memory_space=pltpu.VMEM)
SMEM = pl.BlockSpec(memory_space=pltpu.SMEM)


def per_device(
    n_dev,
    n_group,
    features,
    coords,
    near_pairs,
    parent_two,
    parent_three,
    rates,
    w_near,
    restrict,
    w_two,
    w_three,
    w_four,
    coupling,
    expand,
    w_out,
):
    points_n, channels = features.shape
    points, s_rows = expand.shape
    blocks = points_n // points
    nodes = parent_three.shape[0]
    slots_n = n_dev * SLOTS
    wide_lanes = -(-slots_n // LANES) * LANES
    half_n = n_dev // 2
    wide_rows = s_rows // half_n
    nodes3 = coupling.shape[0] // n_group
    shape = jax.ShapeDtypeStruct
    dma = pltpu.SemaphoreType.DMA
    return pl.pallas_call(
        functools.partial(exchange, n_dev, n_group),
        out_shape=pltpu.VMEM((blocks, points, channels), BF16),
        in_specs=[SMEM, VMEM, ANY] + [VMEM] * 11,
        out_specs=VMEM,
        scratch_shapes=[
            pltpu.VMEM((blocks, points, channels), BF16),
            pltpu.VMEM((ROWS, wide_lanes), jnp.int32),
            pltpu.SMEM((ROWS, wide_lanes), jnp.int32),
            pltpu.VMEM((blocks, points, channels), BF16),
            pltpu.VMEM((blocks, POS, points), F32),
            pltpu.VMEM((blocks, AUG, points), BF16),
            pltpu.VMEM((n_dev, SLOTS, points, channels), BF16),
            pltpu.VMEM((n_dev, SLOTS, points, channels), BF16),
            pltpu.VMEM((n_dev, SLOTS * POS, points), BF16),
            pltpu.VMEM((n_dev, SLOTS * POS, points), BF16),
            pltpu.VMEM((blocks + slots_n, points, channels), F32),
            pltpu.VMEM((blocks, s_rows, channels), F32),
            pltpu.VMEM((s_rows, nodes, channels), BF16),
            pltpu.VMEM((half_n, wide_rows, nodes, channels), BF16),
            pltpu.VMEM((2, wide_rows, nodes, channels), BF16),
            pltpu.VMEM((wide_rows, nodes, channels), F32),
            pltpu.VMEM((wide_rows * nodes, channels), F32),
            pltpu.VMEM((wide_rows * nodes3, channels), BF16),
            pltpu.VMEM((n_group, wide_rows * nodes3, channels), BF16),
            pltpu.VMEM((s_rows, nodes, channels), BF16),
            pltpu.VMEM((blocks, s_rows, channels), F32),
            pltpu.VMEM((blocks, points, channels), F32),
            dma((2, SLOTS * n_dev)),
            dma((2, n_dev)),
            dma((2, n_dev)),
            dma((2, n_group)),
            dma((2, n_dev)),
            dma((2,)),
        ],
        compiler_params=pltpu.CompilerParams(
            collective_id=0, has_side_effects=True, vmem_limit_bytes=60 * 1024 * 1024
        ),
        name="exchange",
    )(
        rates,
        near_pairs,
        features.reshape(blocks, points, channels),
        coords,
        parent_two.reshape(1, -1),
        parent_three.reshape(1, -1),
        w_near,
        restrict,
        w_two,
        w_three,
        w_four,
        coupling,
        expand.T,
        w_out,
    ).reshape(points_n, channels)


def solution(mesh):
    placed = (
        P(("group", "dev"), None),
        P(None, ("group", "dev")),
        P(None, "group"),
        P(("group", "dev")),
        P("group"),
    ) + (P(),) * 9
    return jax.shard_map(
        functools.partial(per_device, mesh.shape["dev"], mesh.shape["group"]),
        mesh=mesh,
        in_specs=placed,
        out_specs=P(("group", "dev"), None),
        check_vma=False,
    )
```

```python
import functools
import math

import jax
import jax.numpy as jnp
from jax import lax
from jax.experimental import pallas as pl
from jax.experimental.pallas import tpu as pltpu
from jax.sharding import PartitionSpec as P

CAP = 2
SLOTS = 2 * CAP
AUG = 16
POS = 4
ROWS = 8
LANES = 128
LOG2E = math.log2(math.e)
MESH = pl.DeviceIdType.MESH
F32 = jnp.float32
BF16 = jnp.bfloat16


def mm(a, b):
    return jnp.dot(a, b, preferred_element_type=F32)


def iota(shape, axis):
    return lax.broadcasted_iota(jnp.int32, shape, axis)


def onehot(mask):
    return mask.astype(F32).astype(BF16)


def find_slots(n_dev, blocks, me, peer_of, turn, pairs):
    pairs_n = pairs.shape[1]
    slots_n = n_dev * SLOTS
    a, b = pairs[0:1], pairs[1:2]

    def slot_and_mask(place):
        remote = place - SLOTS
        slot = jnp.where(remote < 0, place, remote // (n_dev - 1))
        return slot, jnp.where(remote < 0, 0, turn(remote % (n_dev - 1) + 1))

    slot, mask = slot_and_mask(iota((slots_n, 1), 0))
    first = slot < CAP
    here = jnp.where(first, a, b)
    there = jnp.where(first, b, a)
    hit = (here // blocks == me) & (there // blocks == peer_of(mask))
    column = iota((slots_n, pairs_n), 1)
    low = jnp.min(jnp.where(hit, column, pairs_n), axis=1, keepdims=True)
    high = jnp.max(jnp.where(hit, column, -1), axis=1, keepdims=True)
    wanted = jnp.where(slot % CAP == 0, low, jnp.where(high > low, high, pairs_n))
    found = jnp.max(jnp.where(column == wanted, here - me * blocks, -1), axis=1, keepdims=True)

    def to_row(column):
        n = column.shape[0]
        return jnp.max(jnp.where(iota((n, n), 0) == iota((n, n), 1), column, -1), axis=0, keepdims=True)

    found_row = to_row(found)
    place = iota((slots_n, slots_n), 1)
    same = (found_row == found) & (found_row >= 0) & (place < iota((slots_n, slots_n), 0))
    earlier = jnp.max(jnp.where(same, place + blocks, -1), axis=1, keepdims=True)
    prev = jnp.maximum(jnp.where(earlier < 0, found, earlier), 0)
    block = iota((blocks, slots_n), 0)
    last = jnp.where(found_row == block, iota((blocks, slots_n), 1) + blocks, block)
    last = jnp.max(last, axis=1, keepdims=True)
    return jnp.maximum(found_row, 0), to_row(prev), to_row(last)


def augment(xyz):
    norm = jnp.sum(xyz * xyz, axis=0, keepdims=True)
    one = norm.astype(BF16).astype(F32)
    two = (norm - one).astype(BF16).astype(F32)
    three = norm - one - two
    ones = jnp.ones_like(norm)
    return (one, two, three), (ones, ones, ones)


def augment_p(xyz):
    norms, ones = augment(xyz)
    pad = jnp.zeros((AUG - 9, xyz.shape[1]), F32)
    return jnp.concatenate((-2.0 * xyz,) + norms + ones + (pad,), axis=0).astype(BF16)


def augment_q(xyz):
    norms, ones = augment(xyz)
    pad = jnp.zeros((AUG - 9, xyz.shape[1]), F32)
    return jnp.concatenate((xyz,) + ones + norms + (pad,), axis=0).astype(BF16)


def table_apply(pos_p, pos_q, values, rates_ref, heads):
    d2 = lax.dot_general(pos_p, pos_q, (((0,), (0,)), ((), ())), preferred_element_type=F32)
    head_of = iota(values.shape, 1) // (values.shape[1] // heads)
    tables, parts = [], []
    for h in range(heads):
        tables.append(jnp.exp2(d2 * (rates_ref[h] * (-LOG2E))).astype(BF16))
        parts.append(jnp.where(head_of == h, values, jnp.zeros_like(values)))
    return mm(jnp.concatenate(tables, axis=1), jnp.concatenate(parts, axis=0))


def exchange(
    n_dev,
    n_group,
    rates_hbm,
    pairs_hbm,
    feat_hbm,
    coords_hbm,
    par_hbm,
    p3_hbm,
    wnear_hbm,
    restrict_hbm,
    wtwo_hbm,
    wthree_hbm,
    wfour_hbm,
    coupling_hbm,
    expand_hbm,
    wout_hbm,
    out_ref,
    rates_ref,
    pairs_ref,
    feat_ref,
    coords_ref,
    par_ref,
    p3_ref,
    wnear_ref,
    restrict_ref,
    wtwo_ref,
    wthree_ref,
    wfour_ref,
    coupling_ref,
    expand_ref,
    wout_ref,
    table_ref,
    table_smem,
    vals_ref,
    pos4_ref,
    posp_ref,
    send_v,
    got_v,
    send_p,
    got_p,
    running,
    level_ref,
    partial_ref,
    got_part,
    sum_part,
    half_ref,
    lifted_ref,
    three_buf,
    got_three,
    got_down,
    parent_down,
    far_ref,
    v_sems,
    q_sems,
    part_sems,
    three_sems,
    down_sems,
    local_sems,
    in_sems,
):
    me = lax.axis_index("dev")
    mine = lax.axis_index("group")
    heads = rates_hbm.shape[0]
    blocks, points, channels = vals_ref.shape
    s_rows, nodes, _ = partial_ref.shape
    half_n = n_dev // 2
    wide_rows = s_rows // half_n
    nodes3 = coupling_hbm.shape[0] // n_group
    stages = n_dev.bit_length() - 1
    bits = [(me // (1 << t)) % 2 for t in range(stages)]

    def peer_of(mask):
        other = 0
        for t in range(stages):
            flip = (mask // (1 << t)) % 2
            other = other + (bits[t] + flip - 2 * bits[t] * flip) * (1 << t)
        return other

    shift = half_n // 2 * (1 - (bits[-1] + bits[-2]) % 2)

    def turn(k):
        far = half_n + (k - half_n + shift) % half_n
        return jnp.where(k < half_n, k, far)

    def each(fn, low, high):
        def body(k, _):
            fn(k)
            return 0

        lax.fori_loop(low, high, body, 0)

    barrier = pltpu.get_barrier_semaphore()
    each(
        lambda k: pl.semaphore_signal(barrier, inc=1, device_id={"dev": peer_of(k)}, device_id_type=MESH),
        1,
        n_dev,
    )
    each(
        lambda k: pl.semaphore_signal(
            barrier, inc=1, device_id={"group": (mine + k) % n_group}, device_id_type=MESH
        ),
        1,
        n_group,
    )

    loads = [
        pltpu.make_async_copy(source, target, in_sems.at[i])
        for i, (source, target) in enumerate(
            (
                (pairs_hbm, pairs_ref),
                (coords_hbm, coords_ref),
                (feat_hbm, feat_ref),
                (wnear_hbm, wnear_ref),
                (rates_hbm, rates_ref),
                (par_hbm, par_ref),
                (p3_hbm, p3_ref),
                (restrict_hbm, restrict_ref),
                (wtwo_hbm, wtwo_ref),
                (wthree_hbm, wthree_ref),
                (wfour_hbm, wfour_ref),
                (coupling_hbm, coupling_ref),
                (expand_hbm, expand_ref),
                (wout_hbm, wout_ref),
            )
        )
    ]
    for load in loads:
        load.start()

    def dev_copy(src, dst, sems, k, mask):
        return pltpu.make_async_remote_copy(
            src_ref=src,
            dst_ref=dst,
            send_sem=sems.at[0, k],
            recv_sem=sems.at[1, k],
            device_id={"dev": peer_of(mask)},
            device_id_type=MESH,
        )

    mine_rows = pl.ds((me % half_n) * wide_rows, wide_rows)

    def near_copy(mask):
        src = partial_ref.at[pl.ds((peer_of(mask) % half_n) * wide_rows, wide_rows)]
        return dev_copy(src, got_part.at[mask], part_sems, mask, mask)

    def across_copy():
        return dev_copy(sum_part.at[0], sum_part.at[1], part_sems, half_n, half_n)

    def down_copy(mask):
        return dev_copy(got_down.at[mine_rows], got_down.at[mine_rows], down_sems, mask, mask)

    def v_copy(mask, slot):
        return dev_copy(send_v.at[mask, slot], got_v.at[mask, slot], v_sems, slot * n_dev + mask, mask)

    def q_copy(mask):
        return dev_copy(send_p.at[mask], got_p.at[mask], q_sems, mask, mask)

    def three_copy(k):
        return pltpu.make_async_remote_copy(
            src_ref=three_buf,
            dst_ref=got_three.at[mine],
            send_sem=three_sems.at[0, k],
            recv_sem=three_sems.at[1, k],
            device_id={"group": (mine + k) % n_group},
            device_id_type=MESH,
        )

    def feed(slot):
        each(lambda k: v_copy(k, slot).start(), half_n, n_dev)
        each(lambda k: v_copy(k, slot).start(), 1, half_n)

    loads[0].wait()
    found = find_slots(n_dev, blocks, me, peer_of, turn, pairs_ref[...])
    table_ref[...] = jnp.zeros_like(table_ref)
    for i, row in enumerate(found):
        table_ref[i : i + 1, : row.shape[1]] = row
    table_copy = pltpu.make_async_copy(table_ref, table_smem, local_sems.at[0])
    table_copy.start()

    loads[1].wait()
    for j in range(blocks):
        xyz = coords_ref[:, j * points : (j + 1) * points].astype(F32)
        pos4_ref[j] = jnp.concatenate([xyz, jnp.zeros((POS - 3, points), F32)], axis=0)
        posp_ref[j] = augment_p(xyz)

    table_copy.wait()
    for load in loads[2:]:
        load.wait()

    def place_of(mask, slot):
        return slot if isinstance(mask, int) and mask == 0 else SLOTS + slot * (n_dev - 1) + turn(mask) - 1

    def slot_of(mask, slot):
        return table_smem[0, place_of(mask, (slot + CAP) % SLOTS)]

    def pick_v(mask, slot, to_v):
        to_v[mask, slot] = mm(feat_ref[slot_of(mask, slot)], wnear_ref[...]).astype(BF16)

    def pick_p(mask, to_p):
        to_p[mask] = jnp.concatenate(
            [pos4_ref[slot_of(mask, slot)] for slot in range(SLOTS)], axis=0
        ).astype(BF16)

    each(lambda k: pick_v(k, 0, send_v), half_n, n_dev)
    for j in range(blocks):
        level_ref[j] = mm(restrict_ref[...], feat_ref[j]).astype(BF16).astype(F32)
    rows, cols = ROWS * nodes, blocks * ROWS
    row, col = iota((blocks, cols), 0), iota((blocks, cols), 1)
    par_lane = mm(par_ref[...].astype(F32).astype(BF16), onehot(row == col // ROWS)).astype(jnp.int32)
    row, col = iota((rows, cols), 0), iota((rows, cols), 1)
    spread = onehot((row // nodes == col % ROWS) & (row % nodes == par_lane))
    for c in range(s_rows // ROWS):
        part = level_ref[:, c * ROWS : (c + 1) * ROWS, :].reshape(cols, channels).astype(BF16)
        partial_ref[c * ROWS : (c + 1) * ROWS] = mm(spread, part).astype(BF16).reshape(ROWS, nodes, channels)

    pl.semaphore_wait(barrier, n_dev - 1 + n_group - 1)
    each(lambda k: v_copy(k, 0).start(), half_n, n_dev)
    each(lambda k: near_copy(k).start(), 1, half_n)
    each(lambda k: pick_p(k, send_p), 1, n_dev)
    each(lambda k: q_copy(k).start(), 1, n_dev)
    each(lambda k: pick_v(k, 0, send_v), 1, half_n)
    each(lambda k: v_copy(k, 0).start(), 1, half_n)
    for slot in range(1, SLOTS):
        each(lambda k, slot=slot: pick_v(k, slot, send_v), 1, n_dev)
    for slot in range(SLOTS):
        pick_v(0, slot, got_v)
    pick_p(0, got_p)
    for j in range(blocks):
        vals_ref[j] = mm(feat_ref[j], wnear_ref[...]).astype(BF16)

    def self_table(j, _):
        running[j] = table_apply(posp_ref[j], augment_q(pos4_ref[j][:3]), vals_ref[j], rates_ref, heads)
        return 0

    lax.fori_loop(0, blocks, self_table, 0, unroll=2)

    def side_table(mask, slot, place):
        xyz = got_p[mask].astype(F32)[slot * POS : slot * POS + 3]
        local = table_smem[0, place]
        table = table_apply(posp_ref[local], augment_q(xyz), got_v[mask, slot], rates_ref, heads)
        running[blocks + place] = table + running[table_smem[1, place]]

    for slot in range(SLOTS):
        side_table(0, slot, slot)

    def sides(slot, low, high):
        def body(k):
            mask = turn(k)
            v_copy(mask, slot).wait()
            side_table(mask, slot, SLOTS + slot * (n_dev - 1) + k - 1)

        each(body, low, high)

    each(lambda k: near_copy(k).wait(), 1, half_n)
    own = partial_ref[mine_rows].astype(F32)
    for mask in range(1, half_n):
        own = own + got_part[mask].astype(F32)
    half_ref[...] = own
    sum_part[0] = own.astype(BF16)
    across_copy().start()
    feed(1)
    each(lambda k: q_copy(k).wait(), 1, n_dev)
    sides(0, 1, n_dev)

    rows = wide_rows * nodes
    rows3 = wide_rows * nodes3
    all3 = coupling_ref.shape[0]
    row, col = iota((nodes, rows), 0), iota((nodes, rows), 1)
    p3_lane = mm(p3_ref[...].astype(F32).astype(BF16), onehot(row == col % nodes)).astype(jnp.int32)
    row, col = iota((rows3, rows), 0), iota((rows3, rows), 1)
    select = onehot((row // nodes3 == col // nodes) & (row % nodes3 == p3_lane))
    row, col = iota((rows3, all3), 0), iota((rows3, all3), 1)
    left = mm(onehot(col == mine * nodes3 + row % nodes3), coupling_ref[...]).astype(BF16)
    row, col = iota((all3, n_group * rows3), 0), iota((all3, n_group * rows3), 1)
    right = onehot(row == (col // rows3) * nodes3 + col % nodes3)
    row, col = iota((rows3, n_group * rows3), 0), iota((rows3, n_group * rows3), 1)
    wide = jnp.where(row // nodes3 == (col % rows3) // nodes3, mm(left, right), 0.0).astype(BF16)

    across_copy().wait()
    flat = (half_ref[...] + sum_part[1].astype(F32)).reshape(rows, channels).astype(BF16)
    two = jax.nn.gelu(mm(flat, wtwo_ref[...])).astype(BF16)
    three_buf[...] = (mm(select, two) * (nodes3 / nodes)).astype(BF16)
    each(lambda k: three_copy(k).start(), 1, n_group)
    feed(2)
    got_three[mine] = three_buf[...]
    lifted_ref[...] = mm(two, wfour_ref[...])
    each(lambda k: three_copy(k).wait(), 1, n_group)
    mixed = mm(wide, got_three[...].reshape(n_group * rows3, channels)).astype(BF16)
    down3 = jax.nn.gelu(mm(mixed, wthree_ref[...])).astype(BF16)
    lift = lax.dot_general(select, down3, (((0,), (0,)), ((), ())), preferred_element_type=F32)
    got_down[mine_rows] = (
        jax.nn.gelu(lifted_ref[...] + lift).astype(BF16).reshape(wide_rows, nodes, channels)
    )
    each(lambda k: down_copy(k).start(), 1, half_n)
    feed(3)
    sides(1, 1, n_dev)

    def down_wait(mask):
        pltpu.make_async_remote_copy(
            src_ref=got_down.at[mine_rows],
            dst_ref=got_down.at[pl.ds((peer_of(mask) % half_n) * wide_rows, wide_rows)],
            send_sem=down_sems.at[0, mask],
            recv_sem=down_sems.at[1, mask],
            device_id={"dev": peer_of(mask)},
            device_id_type=MESH,
        ).wait()

    each(down_wait, 1, half_n)
    rows, cols = blocks * ROWS, ROWS * nodes
    row, col = iota((rows, blocks), 0), iota((rows, blocks), 1)
    par_wide = jnp.where(row // ROWS == col, par_ref[...].astype(F32), 0.0)
    par_col = jnp.sum(par_wide, axis=1, keepdims=True).astype(jnp.int32)
    row, col = iota((rows, cols), 0), iota((rows, cols), 1)
    gather = onehot((row % ROWS == col // nodes) & (par_col == col % nodes))
    for c in range(s_rows // ROWS):
        part = got_down[c * ROWS : (c + 1) * ROWS].reshape(cols, channels)
        parent_down[:, c * ROWS : (c + 1) * ROWS, :] = mm(gather, part).reshape(blocks, ROWS, channels)
    wide_expand = expand_ref[...].astype(F32).T.astype(BF16)

    for j in range(blocks):
        far = mm(wide_expand, parent_down[j].astype(BF16)).astype(BF16)
        far_ref[j] = mm(far, wout_ref[...])

    sides(2, 1, n_dev)
    sides(3, 1, n_dev)

    for j in range(blocks):
        total = running[table_smem[2, j]] * (points ** (-0.5)) + far_ref[j]
        out_ref[j] = total.astype(BF16)


ANY = pl.BlockSpec(memory_space=pl.ANY)
VMEM = pl.BlockSpec(memory_space=pltpu.VMEM)
SMEM = pl.BlockSpec(memory_space=pltpu.SMEM)


def per_device(
    n_dev,
    n_group,
    features,
    coords,
    near_pairs,
    parent_two,
    parent_three,
    rates,
    w_near,
    restrict,
    w_two,
    w_three,
    w_four,
    coupling,
    expand,
    w_out,
):
    points_n, channels = features.shape
    points, s_rows = expand.shape
    blocks = points_n // points
    nodes = parent_three.shape[0]
    slots_n = n_dev * SLOTS
    wide_lanes = -(-slots_n // LANES) * LANES
    half_n = n_dev // 2
    wide_rows = s_rows // half_n
    nodes3 = coupling.shape[0] // n_group
    shape = jax.ShapeDtypeStruct
    dma = pltpu.SemaphoreType.DMA
    inputs = (
        rates,
        near_pairs,
        features.reshape(blocks, points, channels),
        coords,
        parent_two.reshape(1, -1),
        parent_three.reshape(1, -1),
        w_near,
        restrict,
        w_two,
        w_three,
        w_four,
        coupling,
        expand.T,
        w_out,
    )
    return pl.pallas_call(
        functools.partial(exchange, n_dev, n_group),
        out_shape=pltpu.VMEM((blocks, points, channels), BF16),
        in_specs=[ANY] * len(inputs),
        out_specs=VMEM,
        scratch_shapes=[pltpu.SMEM(rates.shape, F32)]
        + [pltpu.VMEM(x.shape, x.dtype) for x in inputs[1:]]
        + [
            pltpu.VMEM((ROWS, wide_lanes), jnp.int32),
            pltpu.SMEM((ROWS, wide_lanes), jnp.int32),
            pltpu.VMEM((blocks, points, channels), BF16),
            pltpu.VMEM((blocks, POS, points), F32),
            pltpu.VMEM((blocks, AUG, points), BF16),
            pltpu.VMEM((n_dev, SLOTS, points, channels), BF16),
            pltpu.VMEM((n_dev, SLOTS, points, channels), BF16),
            pltpu.VMEM((n_dev, SLOTS * POS, points), BF16),
            pltpu.VMEM((n_dev, SLOTS * POS, points), BF16),
            pltpu.VMEM((blocks + slots_n, points, channels), F32),
            pltpu.VMEM((blocks, s_rows, channels), F32),
            pltpu.VMEM((s_rows, nodes, channels), BF16),
            pltpu.VMEM((half_n, wide_rows, nodes, channels), BF16),
            pltpu.VMEM((2, wide_rows, nodes, channels), BF16),
            pltpu.VMEM((wide_rows, nodes, channels), F32),
            pltpu.VMEM((wide_rows * nodes, channels), F32),
            pltpu.VMEM((wide_rows * nodes3, channels), BF16),
            pltpu.VMEM((n_group, wide_rows * nodes3, channels), BF16),
            pltpu.VMEM((s_rows, nodes, channels), BF16),
            pltpu.VMEM((blocks, s_rows, channels), F32),
            pltpu.VMEM((blocks, points, channels), F32),
            dma((2, SLOTS * n_dev)),
            dma((2, n_dev)),
            dma((2, n_dev)),
            dma((2, n_group)),
            dma((2, n_dev)),
            dma((1,)),
            dma((len(inputs),)),
        ],
        compiler_params=pltpu.CompilerParams(
            collective_id=0, has_side_effects=True, vmem_limit_bytes=60 * 1024 * 1024
        ),
        name="exchange",
    )(*inputs).reshape(points_n, channels)


def solution(mesh):
    placed = (
        P(("group", "dev"), None),
        P(None, ("group", "dev")),
        P(None, "group"),
        P(("group", "dev")),
        P("group"),
    ) + (P(),) * 9
    return jax.shard_map(
        functools.partial(per_device, mesh.shape["dev"], mesh.shape["group"]),
        mesh=mesh,
        in_specs=placed,
        out_specs=P(("group", "dev"), None),
        check_vma=False,
    )
```

```python
import functools
import math

import jax
import jax.numpy as jnp
from jax import lax
from jax.experimental import pallas as pl
from jax.experimental.pallas import tpu as pltpu
from jax.sharding import PartitionSpec as P

CAP = 2
SLOTS = 2 * CAP
AUG = 16
POS = 4
ROWS = 8
LANES = 128
LOG2E = math.log2(math.e)
MESH = pl.DeviceIdType.MESH
F32 = jnp.float32
BF16 = jnp.bfloat16


def mm(a, b):
    return jnp.dot(a, b, preferred_element_type=F32)


def iota(shape, axis):
    return lax.broadcasted_iota(jnp.int32, shape, axis)


def onehot(mask):
    return mask.astype(F32).astype(BF16)


def find_slots(n_dev, blocks, me, peer_of, turn, pairs):
    pairs_n = pairs.shape[1]
    slots_n = n_dev * SLOTS
    a, b = pairs[0:1], pairs[1:2]

    def slot_and_mask(place):
        remote = place - SLOTS
        slot = jnp.where(remote < 0, place, remote // (n_dev - 1))
        return slot, jnp.where(remote < 0, 0, turn(remote % (n_dev - 1) + 1))

    slot, mask = slot_and_mask(iota((slots_n, 1), 0))
    first = slot < CAP
    here = jnp.where(first, a, b)
    there = jnp.where(first, b, a)
    hit = (here // blocks == me) & (there // blocks == peer_of(mask))
    column = iota((slots_n, pairs_n), 1)
    low = jnp.min(jnp.where(hit, column, pairs_n), axis=1, keepdims=True)
    high = jnp.max(jnp.where(hit, column, -1), axis=1, keepdims=True)
    wanted = jnp.where(slot % CAP == 0, low, jnp.where(high > low, high, pairs_n))
    found = jnp.max(jnp.where(column == wanted, here - me * blocks, -1), axis=1, keepdims=True)

    def to_row(column):
        n = column.shape[0]
        return jnp.max(jnp.where(iota((n, n), 0) == iota((n, n), 1), column, -1), axis=0, keepdims=True)

    found_row = to_row(found)
    place = iota((slots_n, slots_n), 1)
    same = (found_row == found) & (found_row >= 0) & (place < iota((slots_n, slots_n), 0))
    earlier = jnp.max(jnp.where(same, place + blocks, -1), axis=1, keepdims=True)
    prev = jnp.maximum(jnp.where(earlier < 0, found, earlier), 0)
    block = iota((blocks, slots_n), 0)
    last = jnp.where(found_row == block, iota((blocks, slots_n), 1) + blocks, block)
    last = jnp.max(last, axis=1, keepdims=True)
    return jnp.maximum(found_row, 0), to_row(prev), to_row(last)


def augment(xyz):
    norm = jnp.sum(xyz * xyz, axis=0, keepdims=True)
    one = norm.astype(BF16).astype(F32)
    two = (norm - one).astype(BF16).astype(F32)
    three = norm - one - two
    ones = jnp.ones_like(norm)
    return (one, two, three), (ones, ones, ones)


def augment_p(xyz):
    norms, ones = augment(xyz)
    pad = jnp.zeros((AUG - 9, xyz.shape[1]), F32)
    return jnp.concatenate((-2.0 * xyz,) + norms + ones + (pad,), axis=0).astype(BF16)


def augment_q(xyz):
    norms, ones = augment(xyz)
    pad = jnp.zeros((AUG - 9, xyz.shape[1]), F32)
    return jnp.concatenate((xyz,) + ones + norms + (pad,), axis=0).astype(BF16)


def table_apply(pos_p, pos_q, values, rates_ref, heads):
    d2 = lax.dot_general(pos_p, pos_q, (((0,), (0,)), ((), ())), preferred_element_type=F32)
    head_of = iota(values.shape, 1) // (values.shape[1] // heads)
    tables, parts = [], []
    for h in range(heads):
        tables.append(jnp.exp2(d2 * (rates_ref[h] * (-LOG2E))).astype(BF16))
        parts.append(jnp.where(head_of == h, values, jnp.zeros_like(values)))
    return mm(jnp.concatenate(tables, axis=1), jnp.concatenate(parts, axis=0))


def exchange(
    n_dev,
    n_group,
    rates_hbm,
    pairs_hbm,
    feat_hbm,
    coords_hbm,
    par_hbm,
    p3_hbm,
    wnear_hbm,
    restrict_hbm,
    wtwo_hbm,
    wthree_hbm,
    wfour_hbm,
    coupling_hbm,
    expand_hbm,
    wout_hbm,
    out_ref,
    rates_ref,
    pairs_ref,
    feat_ref,
    coords_ref,
    par_ref,
    p3_ref,
    wnear_ref,
    restrict_ref,
    wtwo_ref,
    wthree_ref,
    wfour_ref,
    coupling_ref,
    expand_ref,
    wout_ref,
    table_ref,
    table_smem,
    vals_ref,
    pos4_ref,
    posp_ref,
    send_v,
    got_v,
    send_p,
    got_p,
    running,
    level_ref,
    partial_ref,
    got_part,
    sum_part,
    half_ref,
    lifted_ref,
    three_buf,
    got_three,
    got_down,
    parent_down,
    far_ref,
    v_sems,
    q_sems,
    part_sems,
    three_sems,
    down_sems,
    local_sems,
    in_sems,
):
    me = lax.axis_index("dev")
    mine = lax.axis_index("group")
    heads = rates_hbm.shape[0]
    blocks, points, channels = vals_ref.shape
    s_rows, nodes, _ = partial_ref.shape
    half_n = n_dev // 2
    wide_rows = s_rows // half_n
    nodes3 = coupling_hbm.shape[0] // n_group
    stages = n_dev.bit_length() - 1
    bits = [(me // (1 << t)) % 2 for t in range(stages)]

    def peer_of(mask):
        other = 0
        for t in range(stages):
            flip = (mask // (1 << t)) % 2
            other = other + (bits[t] + flip - 2 * bits[t] * flip) * (1 << t)
        return other

    shift = half_n // 2 * (1 - (bits[-1] + bits[-2]) % 2)

    def turn(k):
        far = half_n + (k - half_n + shift) % half_n
        return jnp.where(k < half_n, k, far)

    def each(fn, low, high):
        def body(k, _):
            fn(k)
            return 0

        lax.fori_loop(low, high, body, 0)

    barrier = pltpu.get_barrier_semaphore()
    each(
        lambda k: pl.semaphore_signal(barrier, inc=1, device_id={"dev": peer_of(k)}, device_id_type=MESH),
        1,
        n_dev,
    )
    each(
        lambda k: pl.semaphore_signal(
            barrier, inc=1, device_id={"group": (mine + k) % n_group}, device_id_type=MESH
        ),
        1,
        n_group,
    )

    loads = [
        pltpu.make_async_copy(source, target, in_sems.at[i])
        for i, (source, target) in enumerate(
            (
                (pairs_hbm, pairs_ref),
                (coords_hbm, coords_ref),
                (feat_hbm, feat_ref),
                (wnear_hbm, wnear_ref),
                (rates_hbm, rates_ref),
                (par_hbm, par_ref),
                (p3_hbm, p3_ref),
                (restrict_hbm, restrict_ref),
                (wtwo_hbm, wtwo_ref),
                (wthree_hbm, wthree_ref),
                (wfour_hbm, wfour_ref),
                (coupling_hbm, coupling_ref),
                (expand_hbm, expand_ref),
                (wout_hbm, wout_ref),
            )
        )
    ]
    for load in loads:
        load.start()

    def dev_copy(src, dst, sems, k, mask):
        return pltpu.make_async_remote_copy(
            src_ref=src,
            dst_ref=dst,
            send_sem=sems.at[0, k],
            recv_sem=sems.at[1, k],
            device_id={"dev": peer_of(mask)},
            device_id_type=MESH,
        )

    mine_rows = pl.ds((me % half_n) * wide_rows, wide_rows)

    def near_copy(mask):
        src = partial_ref.at[pl.ds((peer_of(mask) % half_n) * wide_rows, wide_rows)]
        return dev_copy(src, got_part.at[mask], part_sems, mask, mask)

    def across_copy():
        return dev_copy(sum_part.at[0], sum_part.at[1], part_sems, half_n, half_n)

    def down_copy(mask):
        return dev_copy(got_down.at[mine_rows], got_down.at[mine_rows], down_sems, mask, mask)

    def v_copy(mask, slot):
        return dev_copy(send_v.at[mask, slot], got_v.at[mask, slot], v_sems, slot * n_dev + mask, mask)

    def q_copy(mask):
        return dev_copy(send_p.at[mask], got_p.at[mask], q_sems, mask, mask)

    def three_copy(k):
        return pltpu.make_async_remote_copy(
            src_ref=three_buf,
            dst_ref=got_three.at[mine],
            send_sem=three_sems.at[0, k],
            recv_sem=three_sems.at[1, k],
            device_id={"group": (mine + k) % n_group},
            device_id_type=MESH,
        )

    def send_far(low, high):
        each(lambda i: v_copy(half_n + i % half_n, i // half_n).start(), low, high)

    def send_near(slot):
        each(lambda k: v_copy(k, slot).start(), 1, half_n)

    loads[0].wait()
    found = find_slots(n_dev, blocks, me, peer_of, turn, pairs_ref[...])
    table_ref[...] = jnp.zeros_like(table_ref)
    for i, row in enumerate(found):
        table_ref[i : i + 1, : row.shape[1]] = row
    table_copy = pltpu.make_async_copy(table_ref, table_smem, local_sems.at[0])
    table_copy.start()

    loads[1].wait()
    for j in range(blocks):
        xyz = coords_ref[:, j * points : (j + 1) * points].astype(F32)
        pos4_ref[j] = jnp.concatenate([xyz, jnp.zeros((POS - 3, points), F32)], axis=0)
        posp_ref[j] = augment_p(xyz)

    table_copy.wait()
    for load in loads[2:]:
        load.wait()

    def place_of(mask, slot):
        return slot if isinstance(mask, int) and mask == 0 else SLOTS + slot * (n_dev - 1) + turn(mask) - 1

    def slot_of(mask, slot):
        return table_smem[0, place_of(mask, (slot + CAP) % SLOTS)]

    def pick_v(mask, slot, to_v):
        to_v[mask, slot] = mm(feat_ref[slot_of(mask, slot)], wnear_ref[...]).astype(BF16)

    def pick_p(mask, to_p):
        to_p[mask] = jnp.concatenate(
            [pos4_ref[slot_of(mask, slot)] for slot in range(SLOTS)], axis=0
        ).astype(BF16)

    each(lambda k: pick_v(k, 0, send_v), half_n, n_dev)
    for j in range(blocks):
        level_ref[j] = mm(restrict_ref[...], feat_ref[j]).astype(BF16).astype(F32)
    rows, cols = ROWS * nodes, blocks * ROWS
    row, col = iota((blocks, cols), 0), iota((blocks, cols), 1)
    par_lane = mm(par_ref[...].astype(F32).astype(BF16), onehot(row == col // ROWS)).astype(jnp.int32)
    row, col = iota((rows, cols), 0), iota((rows, cols), 1)
    spread = onehot((row // nodes == col % ROWS) & (row % nodes == par_lane))
    for c in range(s_rows // ROWS):
        part = level_ref[:, c * ROWS : (c + 1) * ROWS, :].reshape(cols, channels).astype(BF16)
        partial_ref[c * ROWS : (c + 1) * ROWS] = mm(spread, part).astype(BF16).reshape(ROWS, nodes, channels)

    pl.semaphore_wait(barrier, n_dev - 1 + n_group - 1)
    send_far(0, half_n)
    each(lambda k: near_copy(k).start(), 1, half_n)
    each(lambda k: pick_p(k, send_p), 1, n_dev)
    each(lambda k: q_copy(k).start(), 1, n_dev)
    each(lambda k: pick_v(k, 0, send_v), 1, half_n)
    for slot in range(1, SLOTS):
        each(lambda k, slot=slot: pick_v(k, slot, send_v), 1, n_dev)
    for slot in range(SLOTS):
        pick_v(0, slot, got_v)
    pick_p(0, got_p)
    for j in range(blocks):
        vals_ref[j] = mm(feat_ref[j], wnear_ref[...]).astype(BF16)

    send_far(half_n, half_n + 1)
    send_near(0)

    def self_table(j, _):
        running[j] = table_apply(posp_ref[j], augment_q(pos4_ref[j][:3]), vals_ref[j], rates_ref, heads)
        return 0

    lax.fori_loop(0, blocks, self_table, 0, unroll=2)

    def side_table(mask, slot, place):
        xyz = got_p[mask].astype(F32)[slot * POS : slot * POS + 3]
        local = table_smem[0, place]
        table = table_apply(posp_ref[local], augment_q(xyz), got_v[mask, slot], rates_ref, heads)
        running[blocks + place] = table + running[table_smem[1, place]]

    for slot in range(SLOTS):
        side_table(0, slot, slot)

    def sides(slot, low, high):
        def body(k):
            mask = turn(k)
            v_copy(mask, slot).wait()
            side_table(mask, slot, SLOTS + slot * (n_dev - 1) + k - 1)

        each(body, low, high)

    each(lambda k: near_copy(k).wait(), 1, half_n)
    own = partial_ref[mine_rows].astype(F32)
    for mask in range(1, half_n):
        own = own + got_part[mask].astype(F32)
    half_ref[...] = own
    sum_part[0] = own.astype(BF16)
    across_copy().start()
    send_far(half_n + 1, 2 * half_n)
    send_near(1)
    each(lambda k: q_copy(k).wait(), 1, n_dev)
    sides(0, 1, n_dev)

    rows = wide_rows * nodes
    rows3 = wide_rows * nodes3
    all3 = coupling_ref.shape[0]
    row, col = iota((nodes, rows), 0), iota((nodes, rows), 1)
    p3_lane = mm(p3_ref[...].astype(F32).astype(BF16), onehot(row == col % nodes)).astype(jnp.int32)
    row, col = iota((rows3, rows), 0), iota((rows3, rows), 1)
    select = onehot((row // nodes3 == col // nodes) & (row % nodes3 == p3_lane))
    row, col = iota((rows3, all3), 0), iota((rows3, all3), 1)
    left = mm(onehot(col == mine * nodes3 + row % nodes3), coupling_ref[...]).astype(BF16)
    row, col = iota((all3, n_group * rows3), 0), iota((all3, n_group * rows3), 1)
    right = onehot(row == (col // rows3) * nodes3 + col % nodes3)
    row, col = iota((rows3, n_group * rows3), 0), iota((rows3, n_group * rows3), 1)
    wide = jnp.where(row // nodes3 == (col % rows3) // nodes3, mm(left, right), 0.0).astype(BF16)

    across_copy().wait()
    flat = (half_ref[...] + sum_part[1].astype(F32)).reshape(rows, channels).astype(BF16)
    two = jax.nn.gelu(mm(flat, wtwo_ref[...])).astype(BF16)
    three_buf[...] = (mm(select, two) * (nodes3 / nodes)).astype(BF16)
    each(lambda k: three_copy(k).start(), 1, n_group)
    send_far(2 * half_n, 3 * half_n)
    send_near(2)
    got_three[mine] = three_buf[...]
    lifted_ref[...] = mm(two, wfour_ref[...])
    each(lambda k: three_copy(k).wait(), 1, n_group)
    mixed = mm(wide, got_three[...].reshape(n_group * rows3, channels)).astype(BF16)
    down3 = jax.nn.gelu(mm(mixed, wthree_ref[...])).astype(BF16)
    lift = lax.dot_general(select, down3, (((0,), (0,)), ((), ())), preferred_element_type=F32)
    got_down[mine_rows] = (
        jax.nn.gelu(lifted_ref[...] + lift).astype(BF16).reshape(wide_rows, nodes, channels)
    )
    each(lambda k: down_copy(k).start(), 1, half_n)
    send_far(3 * half_n, SLOTS * half_n)
    send_near(3)
    sides(1, 1, n_dev)

    sides(2, 1, n_dev)

    def down_wait(mask):
        pltpu.make_async_remote_copy(
            src_ref=got_down.at[mine_rows],
            dst_ref=got_down.at[pl.ds((peer_of(mask) % half_n) * wide_rows, wide_rows)],
            send_sem=down_sems.at[0, mask],
            recv_sem=down_sems.at[1, mask],
            device_id={"dev": peer_of(mask)},
            device_id_type=MESH,
        ).wait()

    each(down_wait, 1, half_n)
    rows, cols = blocks * ROWS, ROWS * nodes
    row, col = iota((rows, blocks), 0), iota((rows, blocks), 1)
    par_wide = jnp.where(row // ROWS == col, par_ref[...].astype(F32), 0.0)
    par_col = jnp.sum(par_wide, axis=1, keepdims=True).astype(jnp.int32)
    row, col = iota((rows, cols), 0), iota((rows, cols), 1)
    gather = onehot((row % ROWS == col // nodes) & (par_col == col % nodes))
    for c in range(s_rows // ROWS):
        part = got_down[c * ROWS : (c + 1) * ROWS].reshape(cols, channels)
        parent_down[:, c * ROWS : (c + 1) * ROWS, :] = mm(gather, part).reshape(blocks, ROWS, channels)
    wide_expand = expand_ref[...].astype(F32).T.astype(BF16)

    for j in range(blocks):
        far = mm(wide_expand, parent_down[j].astype(BF16)).astype(BF16)
        far_ref[j] = mm(far, wout_ref[...])

    sides(3, 1, n_dev)

    for j in range(blocks):
        total = running[table_smem[2, j]] * (points ** (-0.5)) + far_ref[j]
        out_ref[j] = total.astype(BF16)


ANY = pl.BlockSpec(memory_space=pl.ANY)
VMEM = pl.BlockSpec(memory_space=pltpu.VMEM)
SMEM = pl.BlockSpec(memory_space=pltpu.SMEM)


def per_device(
    n_dev,
    n_group,
    features,
    coords,
    near_pairs,
    parent_two,
    parent_three,
    rates,
    w_near,
    restrict,
    w_two,
    w_three,
    w_four,
    coupling,
    expand,
    w_out,
):
    points_n, channels = features.shape
    points, s_rows = expand.shape
    blocks = points_n // points
    nodes = parent_three.shape[0]
    slots_n = n_dev * SLOTS
    wide_lanes = -(-slots_n // LANES) * LANES
    half_n = n_dev // 2
    wide_rows = s_rows // half_n
    nodes3 = coupling.shape[0] // n_group
    shape = jax.ShapeDtypeStruct
    dma = pltpu.SemaphoreType.DMA
    inputs = (
        rates,
        near_pairs,
        features.reshape(blocks, points, channels),
        coords,
        parent_two.reshape(1, -1),
        parent_three.reshape(1, -1),
        w_near,
        restrict,
        w_two,
        w_three,
        w_four,
        coupling,
        expand.T,
        w_out,
    )
    return pl.pallas_call(
        functools.partial(exchange, n_dev, n_group),
        out_shape=pltpu.VMEM((blocks, points, channels), BF16),
        in_specs=[ANY] * len(inputs),
        out_specs=VMEM,
        scratch_shapes=[pltpu.SMEM(rates.shape, F32)]
        + [pltpu.VMEM(x.shape, x.dtype) for x in inputs[1:]]
        + [
            pltpu.VMEM((ROWS, wide_lanes), jnp.int32),
            pltpu.SMEM((ROWS, wide_lanes), jnp.int32),
            pltpu.VMEM((blocks, points, channels), BF16),
            pltpu.VMEM((blocks, POS, points), F32),
            pltpu.VMEM((blocks, AUG, points), BF16),
            pltpu.VMEM((n_dev, SLOTS, points, channels), BF16),
            pltpu.VMEM((n_dev, SLOTS, points, channels), BF16),
            pltpu.VMEM((n_dev, SLOTS * POS, points), BF16),
            pltpu.VMEM((n_dev, SLOTS * POS, points), BF16),
            pltpu.VMEM((blocks + slots_n, points, channels), F32),
            pltpu.VMEM((blocks, s_rows, channels), F32),
            pltpu.VMEM((s_rows, nodes, channels), BF16),
            pltpu.VMEM((half_n, wide_rows, nodes, channels), BF16),
            pltpu.VMEM((2, wide_rows, nodes, channels), BF16),
            pltpu.VMEM((wide_rows, nodes, channels), F32),
            pltpu.VMEM((wide_rows * nodes, channels), F32),
            pltpu.VMEM((wide_rows * nodes3, channels), BF16),
            pltpu.VMEM((n_group, wide_rows * nodes3, channels), BF16),
            pltpu.VMEM((s_rows, nodes, channels), BF16),
            pltpu.VMEM((blocks, s_rows, channels), F32),
            pltpu.VMEM((blocks, points, channels), F32),
            dma((2, SLOTS * n_dev)),
            dma((2, n_dev)),
            dma((2, n_dev)),
            dma((2, n_group)),
            dma((2, n_dev)),
            dma((1,)),
            dma((len(inputs),)),
        ],
        compiler_params=pltpu.CompilerParams(
            collective_id=0, has_side_effects=True, vmem_limit_bytes=60 * 1024 * 1024
        ),
        name="exchange",
    )(*inputs).reshape(points_n, channels)


def solution(mesh):
    placed = (
        P(("group", "dev"), None),
        P(None, ("group", "dev")),
        P(None, "group"),
        P(("group", "dev")),
        P("group"),
    ) + (P(),) * 9
    return jax.shard_map(
        functools.partial(per_device, mesh.shape["dev"], mesh.shape["group"]),
        mesh=mesh,
        in_specs=placed,
        out_specs=P(("group", "dev"), None),
        check_vma=False,
    )
```

```python
import functools
import math

import jax
import jax.numpy as jnp
from jax import lax
from jax.experimental import pallas as pl
from jax.experimental.pallas import tpu as pltpu
from jax.sharding import PartitionSpec as P

CAP = 2
SLOTS = 2 * CAP
AUG = 16
POS = 4
ROWS = 8
LANES = 128
LOG2E = math.log2(math.e)
MESH = pl.DeviceIdType.MESH
F32 = jnp.float32
BF16 = jnp.bfloat16


def mm(a, b):
    return jnp.dot(a, b, preferred_element_type=F32)


def iota(shape, axis):
    return lax.broadcasted_iota(jnp.int32, shape, axis)


def onehot(mask):
    return mask.astype(F32).astype(BF16)


def find_slots(n_dev, blocks, me, peer_of, turn, pairs):
    pairs_n = pairs.shape[1]
    slots_n = n_dev * SLOTS
    a, b = pairs[0:1], pairs[1:2]

    def slot_and_mask(place):
        remote = place - SLOTS
        slot = jnp.where(remote < 0, place, remote // (n_dev - 1))
        return slot, jnp.where(remote < 0, 0, turn(remote % (n_dev - 1) + 1))

    slot, mask = slot_and_mask(iota((slots_n, 1), 0))
    first = slot < CAP
    here = jnp.where(first, a, b)
    there = jnp.where(first, b, a)
    hit = (here // blocks == me) & (there // blocks == peer_of(mask))
    column = iota((slots_n, pairs_n), 1)
    low = jnp.min(jnp.where(hit, column, pairs_n), axis=1, keepdims=True)
    high = jnp.max(jnp.where(hit, column, -1), axis=1, keepdims=True)
    wanted = jnp.where(slot % CAP == 0, low, jnp.where(high > low, high, pairs_n))
    found = jnp.max(jnp.where(column == wanted, here - me * blocks, -1), axis=1, keepdims=True)

    def to_row(column):
        n = column.shape[0]
        return jnp.max(jnp.where(iota((n, n), 0) == iota((n, n), 1), column, -1), axis=0, keepdims=True)

    found_row = to_row(found)
    place = iota((slots_n, slots_n), 1)
    same = (found_row == found) & (found_row >= 0) & (place < iota((slots_n, slots_n), 0))
    earlier = jnp.max(jnp.where(same, place + blocks, -1), axis=1, keepdims=True)
    prev = jnp.maximum(jnp.where(earlier < 0, found, earlier), 0)
    block = iota((blocks, slots_n), 0)
    last = jnp.where(found_row == block, iota((blocks, slots_n), 1) + blocks, block)
    last = jnp.max(last, axis=1, keepdims=True)
    return jnp.maximum(found_row, 0), to_row(prev), to_row(last)


def augment(xyz):
    norm = jnp.sum(xyz * xyz, axis=0, keepdims=True)
    one = norm.astype(BF16).astype(F32)
    two = (norm - one).astype(BF16).astype(F32)
    three = norm - one - two
    ones = jnp.ones_like(norm)
    return (one, two, three), (ones, ones, ones)


def augment_p(xyz):
    norms, ones = augment(xyz)
    pad = jnp.zeros((AUG - 9, xyz.shape[1]), F32)
    return jnp.concatenate((-2.0 * xyz,) + norms + ones + (pad,), axis=0).astype(BF16)


def augment_q(xyz):
    norms, ones = augment(xyz)
    pad = jnp.zeros((AUG - 9, xyz.shape[1]), F32)
    return jnp.concatenate((xyz,) + ones + norms + (pad,), axis=0).astype(BF16)


def table_apply(pos_p, pos_q, values, rates_ref, heads):
    d2 = lax.dot_general(pos_p, pos_q, (((0,), (0,)), ((), ())), preferred_element_type=F32)
    head_of = iota(values.shape, 1) // (values.shape[1] // heads)
    tables, parts = [], []
    for h in range(heads):
        tables.append(jnp.exp2(d2 * (rates_ref[h] * (-LOG2E))).astype(BF16))
        parts.append(jnp.where(head_of == h, values, jnp.zeros_like(values)))
    return mm(jnp.concatenate(tables, axis=1), jnp.concatenate(parts, axis=0))


def exchange(
    n_dev,
    n_group,
    rates_hbm,
    pairs_hbm,
    feat_hbm,
    coords_hbm,
    par_hbm,
    p3_hbm,
    wnear_hbm,
    restrict_hbm,
    wtwo_hbm,
    wthree_hbm,
    wfour_hbm,
    coupling_hbm,
    expand_hbm,
    wout_hbm,
    out_ref,
    rates_ref,
    pairs_ref,
    feat_ref,
    coords_ref,
    par_ref,
    p3_ref,
    wnear_ref,
    restrict_ref,
    wtwo_ref,
    wthree_ref,
    wfour_ref,
    coupling_ref,
    expand_ref,
    wout_ref,
    table_ref,
    table_smem,
    vals_ref,
    pos4_ref,
    posp_ref,
    send_v,
    got_v,
    send_p,
    got_p,
    running,
    level_ref,
    partial_ref,
    got_part,
    sum_part,
    half_ref,
    lifted_ref,
    three_buf,
    got_three,
    got_down,
    parent_down,
    far_ref,
    v_sems,
    q_sems,
    part_sems,
    three_sems,
    down_sems,
    local_sems,
    in_sems,
):
    me = lax.axis_index("dev")
    mine = lax.axis_index("group")
    heads = rates_hbm.shape[0]
    blocks, points, channels = vals_ref.shape
    s_rows, nodes, _ = partial_ref.shape
    half_n = n_dev // 2
    wide_rows = s_rows // half_n
    nodes3 = coupling_hbm.shape[0] // n_group
    stages = n_dev.bit_length() - 1
    bits = [(me // (1 << t)) % 2 for t in range(stages)]

    def peer_of(mask):
        other = 0
        for t in range(stages):
            flip = (mask // (1 << t)) % 2
            other = other + (bits[t] + flip - 2 * bits[t] * flip) * (1 << t)
        return other

    shift = half_n // 2 * (1 - (bits[-1] + bits[-2]) % 2)

    def turn(k):
        far = half_n + (k - half_n + shift) % half_n
        return jnp.where(k < half_n, k, far)

    def each(fn, low, high):
        def body(k, _):
            fn(k)
            return 0

        lax.fori_loop(low, high, body, 0)

    barrier = pltpu.get_barrier_semaphore()
    each(
        lambda k: pl.semaphore_signal(barrier, inc=1, device_id={"dev": peer_of(k)}, device_id_type=MESH),
        1,
        n_dev,
    )
    each(
        lambda k: pl.semaphore_signal(
            barrier, inc=1, device_id={"group": (mine + k) % n_group}, device_id_type=MESH
        ),
        1,
        n_group,
    )

    loads = [
        pltpu.make_async_copy(source, target, in_sems.at[i])
        for i, (source, target) in enumerate(
            (
                (pairs_hbm, pairs_ref),
                (coords_hbm, coords_ref),
                (feat_hbm, feat_ref),
                (wnear_hbm, wnear_ref),
                (rates_hbm, rates_ref),
                (par_hbm, par_ref),
                (p3_hbm, p3_ref),
                (restrict_hbm, restrict_ref),
                (wtwo_hbm, wtwo_ref),
                (wthree_hbm, wthree_ref),
                (wfour_hbm, wfour_ref),
                (coupling_hbm, coupling_ref),
                (expand_hbm, expand_ref),
                (wout_hbm, wout_ref),
            )
        )
    ]
    for load in loads:
        load.start()

    def dev_copy(src, dst, sems, k, mask):
        return pltpu.make_async_remote_copy(
            src_ref=src,
            dst_ref=dst,
            send_sem=sems.at[0, k],
            recv_sem=sems.at[1, k],
            device_id={"dev": peer_of(mask)},
            device_id_type=MESH,
        )

    mine_rows = pl.ds((me % half_n) * wide_rows, wide_rows)

    def near_copy(mask):
        src = partial_ref.at[pl.ds((peer_of(mask) % half_n) * wide_rows, wide_rows)]
        return dev_copy(src, got_part.at[mask], part_sems, mask, mask)

    def across_copy():
        return dev_copy(sum_part.at[0], sum_part.at[1], part_sems, half_n, half_n)

    def down_copy(mask):
        return dev_copy(got_down.at[mine_rows], got_down.at[mine_rows], down_sems, mask, mask)

    def v_copy(mask, slot):
        return dev_copy(send_v.at[mask, slot], got_v.at[mask, slot], v_sems, slot * n_dev + mask, mask)

    def q_copy(mask):
        return dev_copy(send_p.at[mask], got_p.at[mask], q_sems, mask, mask)

    def three_copy(k):
        return pltpu.make_async_remote_copy(
            src_ref=three_buf,
            dst_ref=got_three.at[mine],
            send_sem=three_sems.at[0, k],
            recv_sem=three_sems.at[1, k],
            device_id={"group": (mine + k) % n_group},
            device_id_type=MESH,
        )

    def send_far(low, high):
        each(lambda i: v_copy(half_n + i % half_n, i // half_n).start(), low, high)

    def send_near(slot):
        each(lambda k: v_copy(k, slot).start(), 1, half_n)

    loads[0].wait()
    found = find_slots(n_dev, blocks, me, peer_of, turn, pairs_ref[...])
    table_ref[...] = jnp.zeros_like(table_ref)
    for i, row in enumerate(found):
        table_ref[i : i + 1, : row.shape[1]] = row
    table_copy = pltpu.make_async_copy(table_ref, table_smem, local_sems.at[0])
    table_copy.start()

    loads[1].wait()
    for j in range(blocks):
        xyz = coords_ref[:, j * points : (j + 1) * points].astype(F32)
        pos4_ref[j] = jnp.concatenate([xyz, jnp.zeros((POS - 3, points), F32)], axis=0)
        posp_ref[j] = augment_p(xyz)

    table_copy.wait()
    for load in loads[2:]:
        load.wait()

    def place_of(mask, slot):
        return slot if isinstance(mask, int) and mask == 0 else SLOTS + slot * (n_dev - 1) + turn(mask) - 1

    def slot_of(mask, slot):
        return table_smem[0, place_of(mask, (slot + CAP) % SLOTS)]

    def pick_v(mask, slot, to_v):
        to_v[mask, slot] = mm(feat_ref[slot_of(mask, slot)], wnear_ref[...]).astype(BF16)

    def pick_p(mask, to_p):
        to_p[mask] = jnp.concatenate(
            [pos4_ref[slot_of(mask, slot)] for slot in range(SLOTS)], axis=0
        ).astype(BF16)

    pl.semaphore_wait(barrier, n_dev - 1 + n_group - 1)

    def first(k):
        pick_v(k, 0, send_v)
        v_copy(k, 0).start()

    each(first, half_n, n_dev)
    for j in range(blocks):
        level_ref[j] = mm(restrict_ref[...], feat_ref[j]).astype(BF16).astype(F32)
    rows, cols = ROWS * nodes, blocks * ROWS
    row, col = iota((blocks, cols), 0), iota((blocks, cols), 1)
    par_lane = mm(par_ref[...].astype(F32).astype(BF16), onehot(row == col // ROWS)).astype(jnp.int32)
    row, col = iota((rows, cols), 0), iota((rows, cols), 1)
    spread = onehot((row // nodes == col % ROWS) & (row % nodes == par_lane))
    for c in range(s_rows // ROWS):
        part = level_ref[:, c * ROWS : (c + 1) * ROWS, :].reshape(cols, channels).astype(BF16)
        partial_ref[c * ROWS : (c + 1) * ROWS] = mm(spread, part).astype(BF16).reshape(ROWS, nodes, channels)

    each(lambda k: near_copy(k).start(), 1, half_n)
    each(lambda k: pick_p(k, send_p), 1, n_dev)
    each(lambda k: q_copy(k).start(), 1, n_dev)
    each(lambda k: pick_v(k, 0, send_v), 1, half_n)
    for slot in range(1, SLOTS):
        each(lambda k, slot=slot: pick_v(k, slot, send_v), 1, n_dev)
    for slot in range(SLOTS):
        pick_v(0, slot, got_v)
    pick_p(0, got_p)
    for j in range(blocks):
        vals_ref[j] = mm(feat_ref[j], wnear_ref[...]).astype(BF16)

    send_far(half_n, half_n + 1)
    send_near(0)

    def self_table(j, _):
        running[j] = table_apply(posp_ref[j], augment_q(pos4_ref[j][:3]), vals_ref[j], rates_ref, heads)
        return 0

    lax.fori_loop(0, blocks, self_table, 0, unroll=2)

    def side_table(mask, slot, place):
        xyz = got_p[mask].astype(F32)[slot * POS : slot * POS + 3]
        local = table_smem[0, place]
        table = table_apply(posp_ref[local], augment_q(xyz), got_v[mask, slot], rates_ref, heads)
        running[blocks + place] = table + running[table_smem[1, place]]

    for slot in range(SLOTS):
        side_table(0, slot, slot)

    def sides(slot, low, high):
        def body(k):
            mask = turn(k)
            v_copy(mask, slot).wait()
            side_table(mask, slot, SLOTS + slot * (n_dev - 1) + k - 1)

        each(body, low, high)

    each(lambda k: near_copy(k).wait(), 1, half_n)
    own = partial_ref[mine_rows].astype(F32)
    for mask in range(1, half_n):
        own = own + got_part[mask].astype(F32)
    half_ref[...] = own
    sum_part[0] = own.astype(BF16)
    across_copy().start()
    send_far(half_n + 1, 2 * half_n)
    send_near(1)
    each(lambda k: q_copy(k).wait(), 1, n_dev)
    sides(0, 1, n_dev)

    rows = wide_rows * nodes
    rows3 = wide_rows * nodes3
    all3 = coupling_ref.shape[0]
    row, col = iota((nodes, rows), 0), iota((nodes, rows), 1)
    p3_lane = mm(p3_ref[...].astype(F32).astype(BF16), onehot(row == col % nodes)).astype(jnp.int32)
    row, col = iota((rows3, rows), 0), iota((rows3, rows), 1)
    select = onehot((row // nodes3 == col // nodes) & (row % nodes3 == p3_lane))
    row, col = iota((rows3, all3), 0), iota((rows3, all3), 1)
    left = mm(onehot(col == mine * nodes3 + row % nodes3), coupling_ref[...]).astype(BF16)
    row, col = iota((all3, n_group * rows3), 0), iota((all3, n_group * rows3), 1)
    right = onehot(row == (col // rows3) * nodes3 + col % nodes3)
    row, col = iota((rows3, n_group * rows3), 0), iota((rows3, n_group * rows3), 1)
    wide = jnp.where(row // nodes3 == (col % rows3) // nodes3, mm(left, right), 0.0).astype(BF16)

    across_copy().wait()
    flat = (half_ref[...] + sum_part[1].astype(F32)).reshape(rows, channels).astype(BF16)
    two = jax.nn.gelu(mm(flat, wtwo_ref[...])).astype(BF16)
    three_buf[...] = (mm(select, two) * (nodes3 / nodes)).astype(BF16)
    each(lambda k: three_copy(k).start(), 1, n_group)
    send_far(2 * half_n, 3 * half_n)
    send_near(2)
    got_three[mine] = three_buf[...]
    lifted_ref[...] = mm(two, wfour_ref[...])
    each(lambda k: three_copy(k).wait(), 1, n_group)
    mixed = mm(wide, got_three[...].reshape(n_group * rows3, channels)).astype(BF16)
    down3 = jax.nn.gelu(mm(mixed, wthree_ref[...])).astype(BF16)
    lift = lax.dot_general(select, down3, (((0,), (0,)), ((), ())), preferred_element_type=F32)
    got_down[mine_rows] = (
        jax.nn.gelu(lifted_ref[...] + lift).astype(BF16).reshape(wide_rows, nodes, channels)
    )
    each(lambda k: down_copy(k).start(), 1, half_n)
    send_far(3 * half_n, SLOTS * half_n)
    send_near(3)
    sides(1, 1, n_dev)

    sides(2, 1, n_dev)

    def down_wait(mask):
        pltpu.make_async_remote_copy(
            src_ref=got_down.at[mine_rows],
            dst_ref=got_down.at[pl.ds((peer_of(mask) % half_n) * wide_rows, wide_rows)],
            send_sem=down_sems.at[0, mask],
            recv_sem=down_sems.at[1, mask],
            device_id={"dev": peer_of(mask)},
            device_id_type=MESH,
        ).wait()

    each(down_wait, 1, half_n)
    rows, cols = blocks * ROWS, ROWS * nodes
    row, col = iota((rows, blocks), 0), iota((rows, blocks), 1)
    par_wide = jnp.where(row // ROWS == col, par_ref[...].astype(F32), 0.0)
    par_col = jnp.sum(par_wide, axis=1, keepdims=True).astype(jnp.int32)
    row, col = iota((rows, cols), 0), iota((rows, cols), 1)
    gather = onehot((row % ROWS == col // nodes) & (par_col == col % nodes))
    for c in range(s_rows // ROWS):
        part = got_down[c * ROWS : (c + 1) * ROWS].reshape(cols, channels)
        parent_down[:, c * ROWS : (c + 1) * ROWS, :] = mm(gather, part).reshape(blocks, ROWS, channels)
    wide_expand = expand_ref[...].astype(F32).T.astype(BF16)

    for j in range(blocks):
        far = mm(wide_expand, parent_down[j].astype(BF16)).astype(BF16)
        far_ref[j] = mm(far, wout_ref[...])

    sides(3, 1, n_dev)

    for j in range(blocks):
        total = running[table_smem[2, j]] * (points ** (-0.5)) + far_ref[j]
        out_ref[j] = total.astype(BF16)


ANY = pl.BlockSpec(memory_space=pl.ANY)
VMEM = pl.BlockSpec(memory_space=pltpu.VMEM)
SMEM = pl.BlockSpec(memory_space=pltpu.SMEM)


def per_device(
    n_dev,
    n_group,
    features,
    coords,
    near_pairs,
    parent_two,
    parent_three,
    rates,
    w_near,
    restrict,
    w_two,
    w_three,
    w_four,
    coupling,
    expand,
    w_out,
):
    points_n, channels = features.shape
    points, s_rows = expand.shape
    blocks = points_n // points
    nodes = parent_three.shape[0]
    slots_n = n_dev * SLOTS
    wide_lanes = -(-slots_n // LANES) * LANES
    half_n = n_dev // 2
    wide_rows = s_rows // half_n
    nodes3 = coupling.shape[0] // n_group
    shape = jax.ShapeDtypeStruct
    dma = pltpu.SemaphoreType.DMA
    inputs = (
        rates,
        near_pairs,
        features.reshape(blocks, points, channels),
        coords,
        parent_two.reshape(1, -1),
        parent_three.reshape(1, -1),
        w_near,
        restrict,
        w_two,
        w_three,
        w_four,
        coupling,
        expand.T,
        w_out,
    )
    return pl.pallas_call(
        functools.partial(exchange, n_dev, n_group),
        out_shape=pltpu.VMEM((blocks, points, channels), BF16),
        in_specs=[ANY] * len(inputs),
        out_specs=VMEM,
        scratch_shapes=[pltpu.SMEM(rates.shape, F32)]
        + [pltpu.VMEM(x.shape, x.dtype) for x in inputs[1:]]
        + [
            pltpu.VMEM((ROWS, wide_lanes), jnp.int32),
            pltpu.SMEM((ROWS, wide_lanes), jnp.int32),
            pltpu.VMEM((blocks, points, channels), BF16),
            pltpu.VMEM((blocks, POS, points), F32),
            pltpu.VMEM((blocks, AUG, points), BF16),
            pltpu.VMEM((n_dev, SLOTS, points, channels), BF16),
            pltpu.VMEM((n_dev, SLOTS, points, channels), BF16),
            pltpu.VMEM((n_dev, SLOTS * POS, points), BF16),
            pltpu.VMEM((n_dev, SLOTS * POS, points), BF16),
            pltpu.VMEM((blocks + slots_n, points, channels), F32),
            pltpu.VMEM((blocks, s_rows, channels), F32),
            pltpu.VMEM((s_rows, nodes, channels), BF16),
            pltpu.VMEM((half_n, wide_rows, nodes, channels), BF16),
            pltpu.VMEM((2, wide_rows, nodes, channels), BF16),
            pltpu.VMEM((wide_rows, nodes, channels), F32),
            pltpu.VMEM((wide_rows * nodes, channels), F32),
            pltpu.VMEM((wide_rows * nodes3, channels), BF16),
            pltpu.VMEM((n_group, wide_rows * nodes3, channels), BF16),
            pltpu.VMEM((s_rows, nodes, channels), BF16),
            pltpu.VMEM((blocks, s_rows, channels), F32),
            pltpu.VMEM((blocks, points, channels), F32),
            dma((2, SLOTS * n_dev)),
            dma((2, n_dev)),
            dma((2, n_dev)),
            dma((2, n_group)),
            dma((2, n_dev)),
            dma((1,)),
            dma((len(inputs),)),
        ],
        compiler_params=pltpu.CompilerParams(
            collective_id=0, has_side_effects=True, vmem_limit_bytes=60 * 1024 * 1024
        ),
        name="exchange",
    )(*inputs).reshape(points_n, channels)


def solution(mesh):
    placed = (
        P(("group", "dev"), None),
        P(None, ("group", "dev")),
        P(None, "group"),
        P(("group", "dev")),
        P("group"),
    ) + (P(),) * 9
    return jax.shard_map(
        functools.partial(per_device, mesh.shape["dev"], mesh.shape["group"]),
        mesh=mesh,
        in_specs=placed,
        out_specs=P(("group", "dev"), None),
        check_vma=False,
    )
```

```python
import functools
import math

import jax
import jax.numpy as jnp
from jax import lax
from jax.experimental import pallas as pl
from jax.experimental.pallas import tpu as pltpu
from jax.sharding import PartitionSpec as P

CAP = 2
SLOTS = 2 * CAP
AUG = 16
POS = 4
ROWS = 8
LANES = 128
LOG2E = math.log2(math.e)
MESH = pl.DeviceIdType.MESH
F32 = jnp.float32
BF16 = jnp.bfloat16


def mm(a, b):
    return jnp.dot(a, b, preferred_element_type=F32)


def iota(shape, axis):
    return lax.broadcasted_iota(jnp.int32, shape, axis)


def onehot(mask):
    return mask.astype(F32).astype(BF16)


def find_slots(n_dev, blocks, me, peer_of, turn, pairs):
    pairs_n = pairs.shape[1]
    slots_n = n_dev * SLOTS
    a, b = pairs[0:1], pairs[1:2]

    def slot_and_mask(place):
        remote = place - SLOTS
        slot = jnp.where(remote < 0, place, remote // (n_dev - 1))
        return slot, jnp.where(remote < 0, 0, turn(remote % (n_dev - 1) + 1))

    slot, mask = slot_and_mask(iota((slots_n, 1), 0))
    first = slot < CAP
    here = jnp.where(first, a, b)
    there = jnp.where(first, b, a)
    hit = (here // blocks == me) & (there // blocks == peer_of(mask))
    column = iota((slots_n, pairs_n), 1)
    low = jnp.min(jnp.where(hit, column, pairs_n), axis=1, keepdims=True)
    high = jnp.max(jnp.where(hit, column, -1), axis=1, keepdims=True)
    wanted = jnp.where(slot % CAP == 0, low, jnp.where(high > low, high, pairs_n))
    found = jnp.max(jnp.where(column == wanted, here - me * blocks, -1), axis=1, keepdims=True)

    def to_row(column):
        n = column.shape[0]
        return jnp.max(jnp.where(iota((n, n), 0) == iota((n, n), 1), column, -1), axis=0, keepdims=True)

    found_row = to_row(found)
    place = iota((slots_n, slots_n), 1)
    same = (found_row == found) & (found_row >= 0) & (place < iota((slots_n, slots_n), 0))
    earlier = jnp.max(jnp.where(same, place + blocks, -1), axis=1, keepdims=True)
    prev = jnp.maximum(jnp.where(earlier < 0, found, earlier), 0)
    block = iota((blocks, slots_n), 0)
    last = jnp.where(found_row == block, iota((blocks, slots_n), 1) + blocks, block)
    last = jnp.max(last, axis=1, keepdims=True)
    return jnp.maximum(found_row, 0), to_row(prev), to_row(last)


def augment(xyz):
    norm = jnp.sum(xyz * xyz, axis=0, keepdims=True)
    one = norm.astype(BF16).astype(F32)
    two = (norm - one).astype(BF16).astype(F32)
    three = norm - one - two
    ones = jnp.ones_like(norm)
    return (one, two, three), (ones, ones, ones)


def augment_p(xyz):
    norms, ones = augment(xyz)
    pad = jnp.zeros((AUG - 9, xyz.shape[1]), F32)
    return jnp.concatenate((-2.0 * xyz,) + norms + ones + (pad,), axis=0).astype(BF16)


def augment_q(xyz):
    norms, ones = augment(xyz)
    pad = jnp.zeros((AUG - 9, xyz.shape[1]), F32)
    return jnp.concatenate((xyz,) + ones + norms + (pad,), axis=0).astype(BF16)


def table_apply(pos_p, pos_q, values, rates_ref, heads):
    d2 = lax.dot_general(pos_p, pos_q, (((0,), (0,)), ((), ())), preferred_element_type=F32)
    head_of = iota(values.shape, 1) // (values.shape[1] // heads)
    tables, parts = [], []
    for h in range(heads):
        tables.append(jnp.exp2(d2 * (rates_ref[h] * (-LOG2E))).astype(BF16))
        parts.append(jnp.where(head_of == h, values, jnp.zeros_like(values)))
    return mm(jnp.concatenate(tables, axis=1), jnp.concatenate(parts, axis=0))


def exchange(
    n_dev,
    n_group,
    rates_hbm,
    pairs_hbm,
    feat_hbm,
    coords_hbm,
    par_hbm,
    p3_hbm,
    wnear_hbm,
    restrict_hbm,
    wtwo_hbm,
    wthree_hbm,
    wfour_hbm,
    coupling_hbm,
    expand_hbm,
    wout_hbm,
    out_ref,
    rates_ref,
    pairs_ref,
    feat_ref,
    coords_ref,
    par_ref,
    p3_ref,
    wnear_ref,
    restrict_ref,
    wtwo_ref,
    wthree_ref,
    wfour_ref,
    coupling_ref,
    expand_ref,
    wout_ref,
    table_ref,
    table_smem,
    vals_ref,
    pos4_ref,
    posp_ref,
    send_v,
    got_v,
    send_p,
    got_p,
    running,
    level_ref,
    got_level,
    parent_ref,
    got_parent,
    sum_part,
    half_ref,
    lifted_ref,
    three_buf,
    got_three,
    got_down,
    parent_down,
    far_ref,
    v_sems,
    q_sems,
    part_sems,
    three_sems,
    down_sems,
    local_sems,
    in_sems,
):
    me = lax.axis_index("dev")
    mine = lax.axis_index("group")
    heads = rates_hbm.shape[0]
    blocks, points, channels = vals_ref.shape
    s_rows, nodes, _ = got_down.shape
    half_n = n_dev // 2
    wide_rows = s_rows // half_n
    nodes3 = coupling_hbm.shape[0] // n_group
    stages = n_dev.bit_length() - 1
    bits = [(me // (1 << t)) % 2 for t in range(stages)]

    def peer_of(mask):
        other = 0
        for t in range(stages):
            flip = (mask // (1 << t)) % 2
            other = other + (bits[t] + flip - 2 * bits[t] * flip) * (1 << t)
        return other

    shift = half_n // 2 * (1 - (bits[-1] + bits[-2]) % 2)

    def turn(k):
        far = half_n + (k - half_n + shift) % half_n
        return jnp.where(k < half_n, k, far)

    def each(fn, low, high):
        def body(k, _):
            fn(k)
            return 0

        lax.fori_loop(low, high, body, 0)

    barrier = pltpu.get_barrier_semaphore()
    each(
        lambda k: pl.semaphore_signal(barrier, inc=1, device_id={"dev": peer_of(k)}, device_id_type=MESH),
        1,
        n_dev,
    )
    each(
        lambda k: pl.semaphore_signal(
            barrier, inc=1, device_id={"group": (mine + k) % n_group}, device_id_type=MESH
        ),
        1,
        n_group,
    )

    loads = [
        pltpu.make_async_copy(source, target, in_sems.at[i])
        for i, (source, target) in enumerate(
            (
                (pairs_hbm, pairs_ref),
                (coords_hbm, coords_ref),
                (feat_hbm, feat_ref),
                (wnear_hbm, wnear_ref),
                (rates_hbm, rates_ref),
                (par_hbm, par_ref),
                (p3_hbm, p3_ref),
                (restrict_hbm, restrict_ref),
                (wtwo_hbm, wtwo_ref),
                (wthree_hbm, wthree_ref),
                (wfour_hbm, wfour_ref),
                (coupling_hbm, coupling_ref),
                (expand_hbm, expand_ref),
                (wout_hbm, wout_ref),
            )
        )
    ]
    for load in loads:
        load.start()

    def dev_copy(src, dst, sems, k, mask):
        return pltpu.make_async_remote_copy(
            src_ref=src,
            dst_ref=dst,
            send_sem=sems.at[0, k],
            recv_sem=sems.at[1, k],
            device_id={"dev": peer_of(mask)},
            device_id_type=MESH,
        )

    mine_rows = pl.ds((me % half_n) * wide_rows, wide_rows)

    def near_copy(mask):
        src = level_ref.at[peer_of(mask) % half_n]
        return dev_copy(src, got_level.at[mask], part_sems, mask, mask)

    def parent_copy(mask):
        return dev_copy(parent_ref, got_parent.at[mask], part_sems, half_n + mask, mask)

    def across_copy():
        return dev_copy(sum_part.at[0], sum_part.at[1], part_sems, half_n, half_n)

    def down_copy(mask):
        return dev_copy(got_down.at[mine_rows], got_down.at[mine_rows], down_sems, mask, mask)

    def v_copy(mask, slot):
        return dev_copy(send_v.at[mask, slot], got_v.at[mask, slot], v_sems, slot * n_dev + mask, mask)

    def q_copy(mask):
        return dev_copy(send_p.at[mask], got_p.at[mask], q_sems, mask, mask)

    def three_copy(k):
        return pltpu.make_async_remote_copy(
            src_ref=three_buf,
            dst_ref=got_three.at[mine],
            send_sem=three_sems.at[0, k],
            recv_sem=three_sems.at[1, k],
            device_id={"group": (mine + k) % n_group},
            device_id_type=MESH,
        )

    def send_far(low, high):
        each(lambda i: v_copy(half_n + i % half_n, i // half_n).start(), low, high)

    def send_near(slot):
        each(lambda k: v_copy(k, slot).start(), 1, half_n)

    loads[0].wait()
    found = find_slots(n_dev, blocks, me, peer_of, turn, pairs_ref[...])
    table_ref[...] = jnp.zeros_like(table_ref)
    for i, row in enumerate(found):
        table_ref[i : i + 1, : row.shape[1]] = row
    table_copy = pltpu.make_async_copy(table_ref, table_smem, local_sems.at[0])
    table_copy.start()

    loads[1].wait()
    for j in range(blocks):
        xyz = coords_ref[:, j * points : (j + 1) * points].astype(F32)
        pos4_ref[j] = jnp.concatenate([xyz, jnp.zeros((POS - 3, points), F32)], axis=0)
        posp_ref[j] = augment_p(xyz)

    table_copy.wait()
    for load in loads[2:]:
        load.wait()

    def place_of(mask, slot):
        return slot if isinstance(mask, int) and mask == 0 else SLOTS + slot * (n_dev - 1) + turn(mask) - 1

    def slot_of(mask, slot):
        return table_smem[0, place_of(mask, (slot + CAP) % SLOTS)]

    def pick_v(mask, slot, to_v):
        to_v[mask, slot] = mm(feat_ref[slot_of(mask, slot)], wnear_ref[...]).astype(BF16)

    def pick_p(mask, to_p):
        to_p[mask] = jnp.concatenate(
            [pos4_ref[slot_of(mask, slot)] for slot in range(SLOTS)], axis=0
        ).astype(BF16)

    pl.semaphore_wait(barrier, n_dev - 1 + n_group - 1)

    def first(k):
        pick_v(k, 0, send_v)
        v_copy(k, 0).start()

    each(first, half_n, n_dev)
    parent_ref[...] = jnp.zeros_like(parent_ref)
    parent_ref[0:1, :blocks] = par_ref[...]
    for j in range(blocks):
        level = mm(restrict_ref[...], feat_ref[j]).astype(BF16).astype(F32)
        for part in range(half_n):
            level_ref[part, j] = level[part * wide_rows : (part + 1) * wide_rows].astype(BF16)
    each(lambda k: near_copy(k).start(), 1, half_n)
    each(lambda k: parent_copy(k).start(), 1, half_n)
    each(lambda k: pick_p(k, send_p), 1, n_dev)
    each(lambda k: q_copy(k).start(), 1, n_dev)
    each(lambda k: pick_v(k, 0, send_v), 1, half_n)
    for slot in range(1, SLOTS):
        each(lambda k, slot=slot: pick_v(k, slot, send_v), 1, n_dev)
    for slot in range(SLOTS):
        pick_v(0, slot, got_v)
    pick_p(0, got_p)
    for j in range(blocks):
        vals_ref[j] = mm(feat_ref[j], wnear_ref[...]).astype(BF16)

    send_far(half_n, half_n + 1)
    send_near(0)

    def self_table(j, _):
        running[j] = table_apply(posp_ref[j], augment_q(pos4_ref[j][:3]), vals_ref[j], rates_ref, heads)
        return 0

    lax.fori_loop(0, blocks, self_table, 0, unroll=2)

    def side_table(mask, slot, place):
        xyz = got_p[mask].astype(F32)[slot * POS : slot * POS + 3]
        local = table_smem[0, place]
        table = table_apply(posp_ref[local], augment_q(xyz), got_v[mask, slot], rates_ref, heads)
        running[blocks + place] = table + running[table_smem[1, place]]

    for slot in range(SLOTS):
        side_table(0, slot, slot)

    def sides(slot, low, high):
        def body(k):
            mask = turn(k)
            v_copy(mask, slot).wait()
            side_table(mask, slot, SLOTS + slot * (n_dev - 1) + k - 1)

        each(body, low, high)

    each(lambda k: near_copy(k).wait(), 1, half_n)
    each(lambda k: parent_copy(k).wait(), 1, half_n)
    got_level[0] = level_ref[me % half_n]
    got_parent[0] = parent_ref[...]
    chunk = min(ROWS, wide_rows)
    rows, cols = chunk * nodes, blocks * chunk
    for c in range(wide_rows // chunk):
        total = None
        for mask in range(half_n):
            row, col = iota((blocks, cols), 0), iota((blocks, cols), 1)
            parents = got_parent[mask][0:1, :blocks].astype(F32).astype(BF16)
            par_lane = mm(parents, onehot(row == col // chunk)).astype(jnp.int32)
            row, col = iota((rows, cols), 0), iota((rows, cols), 1)
            spread = onehot((row // nodes == col % chunk) & (row % nodes == par_lane))
            part = got_level[mask].astype(F32)[:, c * chunk : (c + 1) * chunk, :]
            term = mm(spread, part.reshape(cols, channels).astype(BF16))
            total = term if total is None else total + term
        total = total.reshape(chunk, nodes, channels)
        half_ref[c * chunk : (c + 1) * chunk] = total
        sum_part[0, c * chunk : (c + 1) * chunk] = total.astype(BF16)
    across_copy().start()
    send_far(half_n + 1, 2 * half_n)
    send_near(1)
    each(lambda k: q_copy(k).wait(), 1, n_dev)
    sides(0, 1, n_dev)

    rows = wide_rows * nodes
    rows3 = wide_rows * nodes3
    all3 = coupling_ref.shape[0]
    row, col = iota((nodes, rows), 0), iota((nodes, rows), 1)
    p3_lane = mm(p3_ref[...].astype(F32).astype(BF16), onehot(row == col % nodes)).astype(jnp.int32)
    row, col = iota((rows3, rows), 0), iota((rows3, rows), 1)
    select = onehot((row // nodes3 == col // nodes) & (row % nodes3 == p3_lane))
    row, col = iota((rows3, all3), 0), iota((rows3, all3), 1)
    left = mm(onehot(col == mine * nodes3 + row % nodes3), coupling_ref[...]).astype(BF16)
    row, col = iota((all3, n_group * rows3), 0), iota((all3, n_group * rows3), 1)
    right = onehot(row == (col // rows3) * nodes3 + col % nodes3)
    row, col = iota((rows3, n_group * rows3), 0), iota((rows3, n_group * rows3), 1)
    wide = jnp.where(row // nodes3 == (col % rows3) // nodes3, mm(left, right), 0.0).astype(BF16)

    across_copy().wait()
    flat = (half_ref[...] + sum_part[1].astype(F32)).reshape(rows, channels).astype(BF16)
    two = jax.nn.gelu(mm(flat, wtwo_ref[...])).astype(BF16)
    three_buf[...] = (mm(select, two) * (nodes3 / nodes)).astype(BF16)
    each(lambda k: three_copy(k).start(), 1, n_group)
    send_far(2 * half_n, 3 * half_n)
    send_near(2)
    got_three[mine] = three_buf[...]
    lifted_ref[...] = mm(two, wfour_ref[...])
    each(lambda k: three_copy(k).wait(), 1, n_group)
    mixed = mm(wide, got_three[...].reshape(n_group * rows3, channels)).astype(BF16)
    down3 = jax.nn.gelu(mm(mixed, wthree_ref[...])).astype(BF16)
    lift = lax.dot_general(select, down3, (((0,), (0,)), ((), ())), preferred_element_type=F32)
    got_down[mine_rows] = (
        jax.nn.gelu(lifted_ref[...] + lift).astype(BF16).reshape(wide_rows, nodes, channels)
    )
    each(lambda k: down_copy(k).start(), 1, half_n)
    send_far(3 * half_n, SLOTS * half_n)
    send_near(3)
    sides(1, 1, n_dev)

    sides(2, 1, n_dev)

    def down_wait(mask):
        pltpu.make_async_remote_copy(
            src_ref=got_down.at[mine_rows],
            dst_ref=got_down.at[pl.ds((peer_of(mask) % half_n) * wide_rows, wide_rows)],
            send_sem=down_sems.at[0, mask],
            recv_sem=down_sems.at[1, mask],
            device_id={"dev": peer_of(mask)},
            device_id_type=MESH,
        ).wait()

    each(down_wait, 1, half_n)
    rows, cols = blocks * ROWS, ROWS * nodes
    row, col = iota((rows, blocks), 0), iota((rows, blocks), 1)
    par_wide = jnp.where(row // ROWS == col, par_ref[...].astype(F32), 0.0)
    par_col = jnp.sum(par_wide, axis=1, keepdims=True).astype(jnp.int32)
    row, col = iota((rows, cols), 0), iota((rows, cols), 1)
    gather = onehot((row % ROWS == col // nodes) & (par_col == col % nodes))
    for c in range(s_rows // ROWS):
        part = got_down[c * ROWS : (c + 1) * ROWS].reshape(cols, channels)
        parent_down[:, c * ROWS : (c + 1) * ROWS, :] = mm(gather, part).reshape(blocks, ROWS, channels)
    wide_expand = expand_ref[...].astype(F32).T.astype(BF16)

    for j in range(blocks):
        far = mm(wide_expand, parent_down[j].astype(BF16)).astype(BF16)
        far_ref[j] = mm(far, wout_ref[...])

    sides(3, 1, n_dev)

    for j in range(blocks):
        total = running[table_smem[2, j]] * (points ** (-0.5)) + far_ref[j]
        out_ref[j] = total.astype(BF16)


ANY = pl.BlockSpec(memory_space=pl.ANY)
VMEM = pl.BlockSpec(memory_space=pltpu.VMEM)
SMEM = pl.BlockSpec(memory_space=pltpu.SMEM)


def per_device(
    n_dev,
    n_group,
    features,
    coords,
    near_pairs,
    parent_two,
    parent_three,
    rates,
    w_near,
    restrict,
    w_two,
    w_three,
    w_four,
    coupling,
    expand,
    w_out,
):
    points_n, channels = features.shape
    points, s_rows = expand.shape
    blocks = points_n // points
    nodes = parent_three.shape[0]
    slots_n = n_dev * SLOTS
    wide_lanes = -(-slots_n // LANES) * LANES
    half_n = n_dev // 2
    wide_rows = s_rows // half_n
    nodes3 = coupling.shape[0] // n_group
    shape = jax.ShapeDtypeStruct
    dma = pltpu.SemaphoreType.DMA
    inputs = (
        rates,
        near_pairs,
        features.reshape(blocks, points, channels),
        coords,
        parent_two.reshape(1, -1),
        parent_three.reshape(1, -1),
        w_near,
        restrict,
        w_two,
        w_three,
        w_four,
        coupling,
        expand.T,
        w_out,
    )
    return pl.pallas_call(
        functools.partial(exchange, n_dev, n_group),
        out_shape=pltpu.VMEM((blocks, points, channels), BF16),
        in_specs=[ANY] * len(inputs),
        out_specs=VMEM,
        scratch_shapes=[pltpu.SMEM(rates.shape, F32)]
        + [pltpu.VMEM(x.shape, x.dtype) for x in inputs[1:]]
        + [
            pltpu.VMEM((ROWS, wide_lanes), jnp.int32),
            pltpu.SMEM((ROWS, wide_lanes), jnp.int32),
            pltpu.VMEM((blocks, points, channels), BF16),
            pltpu.VMEM((blocks, POS, points), F32),
            pltpu.VMEM((blocks, AUG, points), BF16),
            pltpu.VMEM((n_dev, SLOTS, points, channels), BF16),
            pltpu.VMEM((n_dev, SLOTS, points, channels), BF16),
            pltpu.VMEM((n_dev, SLOTS * POS, points), BF16),
            pltpu.VMEM((n_dev, SLOTS * POS, points), BF16),
            pltpu.VMEM((blocks + slots_n, points, channels), F32),
            pltpu.VMEM((half_n, blocks, wide_rows, channels), BF16),
            pltpu.VMEM((half_n, blocks, wide_rows, channels), BF16),
            pltpu.VMEM((ROWS, LANES), jnp.int32),
            pltpu.VMEM((half_n, ROWS, LANES), jnp.int32),
            pltpu.VMEM((2, wide_rows, nodes, channels), BF16),
            pltpu.VMEM((wide_rows, nodes, channels), F32),
            pltpu.VMEM((wide_rows * nodes, channels), F32),
            pltpu.VMEM((wide_rows * nodes3, channels), BF16),
            pltpu.VMEM((n_group, wide_rows * nodes3, channels), BF16),
            pltpu.VMEM((s_rows, nodes, channels), BF16),
            pltpu.VMEM((blocks, s_rows, channels), F32),
            pltpu.VMEM((blocks, points, channels), F32),
            dma((2, SLOTS * n_dev)),
            dma((2, n_dev)),
            dma((2, n_dev)),
            dma((2, n_group)),
            dma((2, n_dev)),
            dma((1,)),
            dma((len(inputs),)),
        ],
        compiler_params=pltpu.CompilerParams(
            collective_id=0, has_side_effects=True, vmem_limit_bytes=60 * 1024 * 1024
        ),
        name="exchange",
    )(*inputs).reshape(points_n, channels)


def solution(mesh):
    placed = (
        P(("group", "dev"), None),
        P(None, ("group", "dev")),
        P(None, "group"),
        P(("group", "dev")),
        P("group"),
    ) + (P(),) * 9
    return jax.shard_map(
        functools.partial(per_device, mesh.shape["dev"], mesh.shape["group"]),
        mesh=mesh,
        in_specs=placed,
        out_specs=P(("group", "dev"), None),
        check_vma=False,
    )
```
